32 devices in a mesh: group: 2 (over x), row: 16 (over z, y, core), feat: 1.
Axes of the slice: x: 2, y: 2, z: 4, core: 2. Of those that a mesh axis runs over, the one named last changes fastest.
Arguments:
- cells: bfloat16 [1024, 256, 128], P(('group', 'row'), 'feat'), parts along dimension 0, may hold values from -6 to 6
- is_context: int32 [1024], P(('group', 'row')), parts along dimension 0, may hold values from 0 to 1, as said below
- labels: int32 [1024], P(('group', 'row', 'feat')), parts along dimension 0, may hold values from 0 to 9
- inducing: bfloat16 [96, 128], replicated, may hold values from -6 to 6
- induce_query: bfloat16 [128, 128], replicated, may hold values from -1.5 to 1.5
- column_kvo: bfloat16 [3, 128, 128], replicated, may hold values from -0.5 to 0.5
- cell_qkvo: bfloat16 [4, 128, 128], replicated, may hold values from -0.5 to 0.5
- class_tokens: bfloat16 [4, 128], replicated, may hold values from -6 to 6
- class_query: bfloat16 [128, 128], replicated, may hold values from -1.5 to 1.5
- row_kvo: bfloat16 [3, 128, 128], replicated, may hold values from -0.5 to 0.5
- label_table: bfloat16 [10, 512], replicated, may hold values from -6 to 6
- icl_query: bfloat16 [512, 512], replicated, may hold values from -0.75 to 0.75
- icl_kvo: bfloat16 [3, 512, 512], replicated, may hold values from -0.25 to 0.25
Outputs:
- row_outputs: bfloat16 [1024, 512], P(('group', 'row', 'feat')), parts along dimension 0
The draws below stay inside these ranges and needn't reach their ends.
There are 2 independent parts, one for each index of `group`. The reference program is written for one: setup_inputs(seed, part) draws one part's arguments, and reference() takes and returns one part's arrays. A program takes and returns all parts, laid end to end along the dimension named above; an argument that names none is the same for every part. Nothing has to cross between parts.
Inputs may be any that keep to these rules, and one draw needn't show every extreme that they name: `is_context`: 1 marks a labelled context row, 0 a query row; every window holds context rows.
All inputs are finite; a program needn't handle non-finite values.
Results may differ from the reference program's by a relative error of at most 0.017.
Values may be sent and summed in bfloat16 or wider, within the bound.
No kernel may reach another device: no remote copies, remote signals or barrier semaphores. Data moves between devices by JAX's collectives and lax.ppermute only.
A program may use at most 128 MiB of HBM per device.

```python
import math
import jax
import jax.numpy as jnp
from jax import lax

CELL_WIDTH = 128
F = 256
M = 96
HEADS = 4
ROW_HEADS = 8
CLS = 4
C = 10
R_DEV = 32
WINDOW_ROWS = 512
DH = 32
DF = 16
D3 = 512
DR = 128


def draw_is_context(key, part):
    start_key = jax.random.fold_in(key, 11)
    flag_key = jax.random.fold_in(key, 23)
    run_length = max(2 * R_DEV, WINDOW_ROWS // 4)
    run_start = jax.random.randint(start_key, (), 0, WINDOW_ROWS - run_length + 1, dtype=jnp.int32)
    positions = jnp.arange(WINDOW_ROWS, dtype=jnp.int32)
    inside = (positions >= run_start) & (positions < run_start + run_length)
    scattered = jax.random.randint(flag_key, (WINDOW_ROWS,), 0, 2, dtype=jnp.int32)
    return jnp.where(inside, jnp.ones_like(scattered), scattered).astype(jnp.int32)


def draw_class_tokens(key, part):
    values = jnp.clip(jax.random.normal(jax.random.fold_in(key, 37), (CLS, CELL_WIDTH), jnp.float32), -6.0, 6.0)
    return values.astype(jnp.bfloat16)


def with_ends(result, own_key, least, largest):
    spot = [jax.random.randint(jax.random.fold_in(own_key, axis), (), 0, length) for axis, length in enumerate(result.shape)]
    main_axis = result.shape.index(max(result.shape))
    next_to = spot[:main_axis] + [(spot[main_axis] + 1) % result.shape[main_axis]] + spot[main_axis + 1:]
    return result.at[tuple(spot)].set(least).at[tuple(next_to)].set(largest)


def block_scale(rng, extent, pieces, least, top_value):
    gain, own = 1.0, jax.random.fold_in(rng, 6)
    for position, shards_of in pieces:
        heights = jnp.exp(jax.random.uniform(jax.random.fold_in(own, position), (shards_of,), jnp.float32, least / len(pieces), top_value / len(pieces)))
        gain = gain * jnp.repeat(heights, extent[position] // shards_of).reshape([-1 if axis == position else 1 for axis in range(len(extent))])
    return gain


def noise(key, extent, scale, bound, split=(), kind=jnp.bfloat16):
    gain = block_scale(key, extent, split, -0.22, 0.18) if split else 1.0
    result = jax.random.normal(key, extent, jnp.float32) * scale * gain
    return jnp.minimum(jnp.maximum(result, -bound), bound).astype(kind)


def setup_inputs(seed: int = 0, part: int = 0) -> dict:
    key_of = jax.random.split(jax.random.key(seed), 14)
    part_splits = jax.random.split(jax.random.fold_in(key_of[13], part), 14)
    cells = noise(part_splits[0], (WINDOW_ROWS, F, CELL_WIDTH), 1.0, 6.0, ((0, 16),))
    is_context = draw_is_context(jax.random.fold_in(jax.random.fold_in(key_of[13], part), 71), part)
    labels = with_ends(jax.random.randint(part_splits[2], (WINDOW_ROWS,), 0, C), jax.random.fold_in(part_splits[2], 1), 0, C - 1).astype(jnp.int32)
    inducing = noise(key_of[3], (M, CELL_WIDTH), 1.0, 6.0)
    induce_query = noise(key_of[4], (CELL_WIDTH, CELL_WIDTH), (CELL_WIDTH // 9) ** -0.5, 1.5)
    column_kvo = noise(key_of[5], (3, CELL_WIDTH, CELL_WIDTH), CELL_WIDTH ** -0.5, 0.5)
    cell_qkvo = noise(key_of[6], (4, CELL_WIDTH, CELL_WIDTH), CELL_WIDTH ** -0.5, 0.5)
    class_tokens = draw_class_tokens(jax.random.fold_in(key_of[13], 71), part)
    class_query = noise(key_of[8], (CELL_WIDTH, CELL_WIDTH), (CELL_WIDTH // 9) ** -0.5, 1.5)
    row_kvo = noise(key_of[9], (3, CELL_WIDTH, CELL_WIDTH), CELL_WIDTH ** -0.5, 0.5)
    label_table = noise(key_of[10], (C, D3), 1.0, 6.0)
    icl_query = noise(key_of[11], (D3, D3), (D3 // 9) ** -0.5, 0.75)
    icl_kvo = noise(key_of[12], (3, D3, D3), D3 ** -0.5, 0.25)
    return {"cells": cells, "is_context": is_context, "labels": labels, "inducing": inducing, "induce_query": induce_query, "column_kvo": column_kvo, "cell_qkvo": cell_qkvo, "class_tokens": class_tokens, "class_query": class_query, "row_kvo": row_kvo, "label_table": label_table, "icl_query": icl_query, "icl_kvo": icl_kvo}


epsilon = 1e-06

def narrow_precision(value):
    return lax.optimization_barrier(value.astype(jnp.bfloat16))

def promote_precision(value):
    return value.astype(jnp.float32)

def reference(cells, is_context, labels, inducing, induce_query, column_kvo, cell_qkvo, class_tokens, class_query, row_kvo, label_table, icl_query, icl_kvo):
    context_rows = (is_context == 1).astype(jnp.float32)
    scale_factor = 1.0 / math.sqrt(DH)
    feat_scaling = 1.0 / math.sqrt(DF)
    inducing_query = promote_precision(narrow_precision(jnp.dot(inducing, induce_query, preferred_element_type=jnp.float32))).reshape(M, HEADS, DH)
    cls_query = promote_precision(narrow_precision(jnp.dot(class_tokens, class_query, preferred_element_type=jnp.float32))).reshape(CLS, ROW_HEADS, DF)
    cls_keys = promote_precision(narrow_precision(jnp.dot(class_tokens, row_kvo[0], preferred_element_type=jnp.float32))).reshape(CLS, ROW_HEADS, DF)
    cls_values = promote_precision(narrow_precision(jnp.dot(class_tokens, row_kvo[1], preferred_element_type=jnp.float32))).reshape(CLS, ROW_HEADS, DF)
    cls_weight = jnp.exp(jnp.einsum('chd,khd->chk', cls_query, cls_keys) * feat_scaling)
    cls_denom = lax.optimization_barrier(jnp.sum(cls_weight, axis=-1))
    cls_numer = jnp.einsum('chk,khd->chd', promote_precision(narrow_precision(cls_weight)), cls_values)

    def feature_step(running, column):
        column_keys = promote_precision(narrow_precision(jnp.dot(column, column_kvo[0], preferred_element_type=jnp.float32))).reshape(WINDOW_ROWS, HEADS, DH)
        column_values = promote_precision(narrow_precision(jnp.dot(column, column_kvo[1], preferred_element_type=jnp.float32))).reshape(WINDOW_ROWS, HEADS, DH)
        column_weight = jnp.exp(jnp.einsum('ysu,jsu->syj', inducing_query, column_keys) * scale_factor) * context_rows[None, None, :]
        col_denom = lax.optimization_barrier(jnp.sum(column_weight, axis=-1))
        column_numerator = jnp.einsum('bka,abu->kbu', promote_precision(narrow_precision(column_weight)), column_values)
        col_mix = narrow_precision(column_numerator / jnp.transpose(col_denom)[:, :, None]).reshape(M, CELL_WIDTH)
        summary = narrow_precision(promote_precision(inducing) + jnp.dot(col_mix, column_kvo[2], preferred_element_type=jnp.float32))
        cell_query_rows = promote_precision(narrow_precision(jnp.dot(column, cell_qkvo[0], preferred_element_type=jnp.float32))).reshape(WINDOW_ROWS, HEADS, DH)
        summary_keys = promote_precision(narrow_precision(jnp.dot(summary, cell_qkvo[1], preferred_element_type=jnp.float32))).reshape(M, HEADS, DH)
        summary_values = promote_precision(narrow_precision(jnp.dot(summary, cell_qkvo[2], preferred_element_type=jnp.float32))).reshape(M, HEADS, DH)
        unscaled_weight = jnp.exp(jnp.einsum('gie,jie->ijg', cell_query_rows, summary_keys) * scale_factor)
        cell_weight_matrix = promote_precision(narrow_precision(unscaled_weight / lax.optimization_barrier(jnp.sum(unscaled_weight, axis=1, keepdims=True))))
        cell_blend = narrow_precision(jnp.einsum('agb,gav->bav', cell_weight_matrix, summary_values)).reshape(WINDOW_ROWS, CELL_WIDTH)
        column_out = promote_precision(column) + jnp.dot(cell_blend, cell_qkvo[3], preferred_element_type=jnp.float32)
        embedded = narrow_precision(column_out * lax.rsqrt(lax.optimization_barrier(jnp.mean(column_out * column_out, axis=-1, keepdims=True)) + epsilon))
        cell_keys = promote_precision(narrow_precision(jnp.dot(embedded, row_kvo[0], preferred_element_type=jnp.float32))).reshape(WINDOW_ROWS, ROW_HEADS, DF)
        cell_values = promote_precision(narrow_precision(jnp.dot(embedded, row_kvo[1], preferred_element_type=jnp.float32))).reshape(WINDOW_ROWS, ROW_HEADS, DF)
        row_weight = jnp.exp(jnp.einsum('chd,rhd->rch', cls_query, cell_keys) * feat_scaling)
        row_numer, row_denom = running
        row_numer = row_numer + jnp.einsum('rch,rhd->rchd', promote_precision(narrow_precision(row_weight)), cell_values)
        return ((row_numer, row_denom + row_weight), None)
    start_zero = (jnp.zeros((WINDOW_ROWS, CLS, ROW_HEADS, DF), jnp.float32), jnp.zeros((WINDOW_ROWS, CLS, ROW_HEADS), jnp.float32))
    (row_numer, row_denom), _ = lax.scan(feature_step, start_zero, jnp.transpose(cells, (1, 0, 2)))
    row_numer = row_numer + cls_numer[None]
    row_denom = row_denom + cls_denom[None]
    row_mix = narrow_precision(row_numer / row_denom[..., None]).reshape(WINDOW_ROWS * CLS, CELL_WIDTH)
    row_embed = narrow_precision(promote_precision(class_tokens)[None] + jnp.dot(row_mix, row_kvo[2], preferred_element_type=jnp.float32).reshape(WINDOW_ROWS, CLS, CELL_WIDTH)).reshape(WINDOW_ROWS, D3)
    one_hot = (labels[:, None] == jnp.arange(C, dtype=jnp.int32)[None, :]).astype(jnp.bfloat16)
    label_vec = jnp.dot(one_hot, label_table, preferred_element_type=jnp.float32)
    icl_input = narrow_precision(promote_precision(row_embed) + context_rows[:, None] * label_vec)
    query_rows = promote_precision(narrow_precision(jnp.dot(row_embed, icl_query, preferred_element_type=jnp.float32))).reshape(WINDOW_ROWS, HEADS, DR)
    key_rows = promote_precision(narrow_precision(jnp.dot(icl_input, icl_kvo[0], preferred_element_type=jnp.float32))).reshape(WINDOW_ROWS, HEADS, DR)
    value_rows = promote_precision(narrow_precision(jnp.dot(icl_input, icl_kvo[1], preferred_element_type=jnp.float32))).reshape(WINDOW_ROWS, HEADS, DR)
    row_scaling = 1.0 / math.sqrt(DR)
    query_block = math.gcd(WINDOW_ROWS, 512)

    def block_attend(queries):
        icl_weight = jnp.exp(jnp.einsum('qhd,khd->qhk', queries, key_rows) * row_scaling) * context_rows[None, None, :]
        numer = jnp.einsum('qhk,khd->qhd', promote_precision(narrow_precision(icl_weight)), value_rows)
        return narrow_precision(numer / lax.optimization_barrier(jnp.sum(icl_weight, axis=-1))[..., None])
    icl_mix = lax.map(block_attend, query_rows.reshape(WINDOW_ROWS // query_block, query_block, HEADS, DR)).reshape(WINDOW_ROWS, D3)
    return (promote_precision(row_embed) + jnp.dot(icl_mix, icl_kvo[2], preferred_element_type=jnp.float32)).astype(jnp.bfloat16)
```

```python
import functools
import math

import jax
import jax.numpy as jnp
from jax import lax
from jax.experimental import pallas as pl
from jax.experimental.pallas import tpu as pltpu
from jax.sharding import PartitionSpec as P

HEADS = 4
ROW_HEADS = 8
EPSILON = 1e-06
LOG2E = math.log2(math.e)
F32 = jnp.float32
BF16 = jnp.bfloat16
NT = (((1,), (1,)), ((), ()))
TN = (((0,), (0,)), ((), ()))


def dot(a, b):
    return jnp.dot(a, b, preferred_element_type=F32)


def dot_nt(a, b):
    return lax.dot_general(a, b, NT, preferred_element_type=F32)


def head_rows(x, heads):
    width = x.shape[-1]
    lane = lax.broadcasted_iota(jnp.int32, x.shape, 1) // (width // heads)
    x = x.astype(F32)
    return jnp.concatenate(
        [jnp.where(lane == h, x, 0.0) for h in range(heads)], axis=0
    ).astype(BF16)


def prep_kernel(
    inducing,
    induce_query,
    column_kvo,
    cell_qkvo,
    class_tokens,
    class_query,
    row_kvo,
    col_q,
    fold,
    fold_base,
    row_qv,
    cls_sums,
):
    n_induce, width = inducing.shape
    scale = LOG2E / math.sqrt(width // HEADS)
    row_scale = LOG2E / math.sqrt(width // ROW_HEADS)
    iq = dot(inducing[...], induce_query[...]).astype(BF16)
    col_q[...] = (dot_nt(head_rows(iq, HEADS), column_kvo[0]) * scale).astype(BF16)
    mixed = dot(head_rows(column_kvo[1], HEADS), column_kvo[2]).astype(BF16)
    both = jnp.concatenate([mixed, inducing[...]], axis=0)
    keys = dot(both, cell_qkvo[1])
    values = dot(both, cell_qkvo[2])
    n_mixed = mixed.shape[0]
    n_both = n_mixed + n_induce
    g = dot_nt(head_rows(keys, HEADS), cell_qkvo[0]) * scale
    o = dot(head_rows(values, HEADS), cell_qkvo[3])
    for h in range(HEADS):
        for part, at in ((g, 0), (o, HEADS * width)):
            block = part[h * n_both : (h + 1) * n_both]
            lanes = slice(at + h * width, at + (h + 1) * width)
            fold[:, lanes] = block[:n_mixed].astype(BF16)
            fold_base[:, lanes] = block[n_mixed:]
    n_class = class_tokens.shape[0]
    tokens = class_tokens[...]
    rq = dot(tokens, class_query[...]).astype(BF16)
    lane = lax.broadcasted_iota(jnp.int32, (ROW_HEADS, width), 1) // (width // ROW_HEADS)
    head = lax.broadcasted_iota(jnp.int32, (ROW_HEADS, width), 0)
    rq32 = rq.astype(F32)
    blocks = jnp.concatenate(
        [jnp.where(lane == head, rq32[c : c + 1], 0.0) for c in range(n_class)], axis=0
    ).astype(BF16)
    row_qv[: n_class * ROW_HEADS] = (dot_nt(blocks, row_kvo[0]) * row_scale).astype(BF16)
    row_qv[n_class * ROW_HEADS :] = row_kvo[1].astype(F32).T.astype(BF16)
    ck = dot(tokens, row_kvo[0]).astype(BF16).astype(F32)
    cv = dot(tokens, row_kvo[1]).astype(BF16).astype(F32)
    same = (
        lax.broadcasted_iota(jnp.int32, (width, width), 0) // (width // ROW_HEADS)
        == lax.broadcasted_iota(jnp.int32, (width, width), 1) // (width // ROW_HEADS)
    ).astype(F32)
    numer = jnp.zeros((n_class, width), F32)
    denom = jnp.zeros((n_class, width), F32)
    for k in range(n_class):
        score = jnp.dot(
            rq32 * ck[k : k + 1], same, precision=lax.Precision.HIGHEST, preferred_element_type=F32
        )
        weight = jnp.exp2(score * row_scale)
        numer = numer + weight * cv[k : k + 1]
        denom = denom + weight
    cls_sums[0] = numer
    cls_sums[1] = denom


def column_kernel(
    n_feat, n_rows, cells, col_q, fold, fold_base, row_qv, partial, mask_row, w_store, v_store
):
    sources, _, width = cells.shape
    n_total = sources * n_rows
    half = n_rows // 2
    n_induce = fold_base.shape[0]
    n_weights = row_qv.shape[0] - width
    n_class = n_weights // ROW_HEADS
    head_width = width // ROW_HEADS

    flags = cells[:, n_feat * n_rows :, :].astype(F32)
    lane = lax.broadcasted_iota(jnp.int32, flags.shape, 2)
    low = lane < width // 2
    turned = pltpu.roll(flags.reshape(sources * half, width), width // 2, 1).reshape(flags.shape)
    mask = jnp.concatenate(
        [jnp.where(low, flags, turned), jnp.where(low, turned, flags)], axis=1
    ).reshape(n_total, width)
    mask_row[...] = mask.T[: mask_row.shape[0]]
    mask = (mask * 0.125).astype(BF16)

    def feature(f, carry):
        start = pl.multiple_of(f * n_rows, n_rows)
        x = cells[:, pl.ds(start, n_rows), :].reshape(n_total, width)
        xt = x.astype(F32).T
        xt_half = xt.astype(BF16)
        p = jnp.exp2(dot(col_q[...], xt_half)).astype(BF16)
        sums = dot(p, jnp.concatenate([x * mask, mask], axis=1))
        y = (sums[:, :width] / sums[:, width:]).astype(BF16)
        y = jnp.concatenate(
            [y[h * n_induce : (h + 1) * n_induce] for h in range(HEADS)], axis=1
        )
        both = dot(y, fold[...]) + fold_base[...]
        g = jnp.concatenate([both[:, h * width : (h + 1) * width] for h in range(HEADS)], axis=0)
        o = jnp.concatenate(
            [both[:, h * width : (h + 1) * width] for h in range(HEADS, 2 * HEADS)], axis=0
        )
        s = jnp.exp2(dot(g.astype(BF16), xt_half))
        weights = []
        for h in range(HEADS):
            part = s[h * n_induce : (h + 1) * n_induce]
            weights.append((part * (1.0 / jnp.sum(part, axis=0, keepdims=True))).astype(BF16))
        out = xt + dot(o.T.astype(BF16), jnp.concatenate(weights, axis=0))
        mean = jnp.sum(out * out, axis=0, keepdims=True) * (1.0 / width)
        e = (out * lax.rsqrt(mean + EPSILON)).astype(BF16)
        wv = dot(row_qv[...], e)
        w_store[f] = jnp.exp2(wv[:n_weights])
        v_store[f] = wv[n_weights:]
        return carry

    lax.fori_loop(0, n_feat, feature, 0)

    step = min(n_total, 512)
    for at in range(0, n_total, step):
        lanes = slice(at, at + step)
        denom = w_store[0, :, lanes]
        for f in range(1, n_feat):
            denom = denom + w_store[f, :, lanes]
        blocks = [[None] * ROW_HEADS for _ in range(n_class)]
        for h in range(ROW_HEADS):

            def add(f, acc):
                v = v_store[f, h * head_width : (h + 1) * head_width, lanes]
                return tuple(
                    acc[c] + w_store[f, pl.ds(c * ROW_HEADS + h, 1), lanes] * v
                    for c in range(n_class)
                )

            zero = jnp.zeros((head_width, step), F32)
            acc = lax.fori_loop(0, n_feat, add, (zero,) * n_class)
            for c in range(n_class):
                blocks[c][h] = acc[c]
        for c in range(n_class):
            partial[lanes, c * width : (c + 1) * width] = (
                jnp.concatenate(blocks[c], axis=0).T.astype(BF16)
            )
        padded = jnp.concatenate([denom, jnp.zeros((width - n_weights, step), F32)], axis=0)
        partial[lanes, n_class * width :] = padded.T.astype(BF16)


def row_kernel(
    parts, flags, labels, cls_sums, class_tokens, row_out, table, icl_query, icl_kvo,
    embed, icl_in, turned_query,
):
    n_class, width = class_tokens.shape
    full = n_class * width
    total = jnp.sum(parts[...].astype(F32), axis=0)
    lane = lax.broadcasted_iota(jnp.int32, (width, full), 1) // (width // ROW_HEADS)
    spread = (lax.broadcasted_iota(jnp.int32, (width, full), 0) == lane).astype(F32)
    denom = jnp.dot(
        total[:, full:], spread, precision=lax.Precision.HIGHEST, preferred_element_type=F32
    )
    pieces = []
    for c in range(n_class):
        lanes = slice(c * width, (c + 1) * width)
        mix = (total[:, lanes] + cls_sums[0, c : c + 1]) / (
            denom[:, lanes] + cls_sums[1, c : c + 1]
        )
        pieces.append(
            class_tokens[c : c + 1].astype(F32) + dot(mix.astype(BF16), row_out[...])
        )
    row_embed = jnp.concatenate(pieces, axis=1).astype(BF16)
    embed[...] = row_embed
    n_rows = labels.shape[1]
    classes = table.shape[0]
    hot = lax.broadcasted_iota(jnp.int32, (classes, n_rows), 0) == labels[...]
    hot = jnp.where(hot & (flags[...] == 1), 1.0, 0.0).astype(F32)
    label = lax.dot_general(hot, table[...].astype(F32), TN, preferred_element_type=F32)
    icl_in[...] = (row_embed.astype(F32) + label).astype(BF16)
    query = dot(row_embed, icl_query[...]).astype(BF16)
    head = full // HEADS
    scale = LOG2E / math.sqrt(head)
    for h in range(HEADS):
        lanes = slice(h * head, (h + 1) * head)
        turned_query[h * n_rows : (h + 1) * n_rows] = (
            dot_nt(query[:, lanes], icl_kvo[0, :, lanes]) * scale
        ).astype(BF16)


def icl_kernel(rows, turned_query, mask_row, embed, icl_kvo, out):
    full = rows.shape[1]
    n_rows = embed.shape[0]
    head = full // HEADS
    s = dot_nt(turned_query[...], rows[...])
    s = jnp.where(mask_row[0:1] > 0.5, s, -1e30)
    p = jnp.exp2(s - jnp.max(s, axis=1, keepdims=True))
    denom = jnp.sum(p, axis=1, keepdims=True)
    y = (dot(p.astype(BF16), rows[...]) / denom).astype(BF16)
    mix = jnp.concatenate(
        [
            dot(y[h * n_rows : (h + 1) * n_rows], icl_kvo[1, :, h * head : (h + 1) * head])
            for h in range(HEADS)
        ],
        axis=1,
    ).astype(BF16)
    out[...] = (embed[...].astype(F32) + dot(mix, icl_kvo[2])).astype(BF16)


def call(kernel, outs, *args, scratch=(), cost=None, name=None):
    return pl.pallas_call(
        kernel,
        out_shape=tuple(jax.ShapeDtypeStruct(s, d) for s, d in outs),
        in_specs=[pl.BlockSpec(memory_space=pltpu.VMEM)] * len(args),
        out_specs=tuple(pl.BlockSpec(memory_space=pltpu.VMEM) for _ in outs),
        scratch_shapes=scratch,
        compiler_params=pltpu.CompilerParams(vmem_limit_bytes=48 * 1024 * 1024),
        name=name,
    )(*args)


def on_device(
    cells,
    is_context,
    labels,
    inducing,
    induce_query,
    column_kvo,
    cell_qkvo,
    class_tokens,
    class_query,
    row_kvo,
    label_table,
    icl_query,
    icl_kvo,
):
    n_rows, n_feat, width = cells.shape
    n_induce = inducing.shape[0]
    n_class = class_tokens.shape[0]
    n_dev = lax.axis_size("row")
    n_split = lax.axis_size("feat")
    own_feat = n_feat // n_dev
    n_total = n_dev * n_rows
    local_rows = n_rows // n_split
    full = n_class * width

    col_q, fold, fold_base, row_qv, cls_sums = call(
        prep_kernel,
        [
            ((HEADS * n_induce, width), BF16),
            ((HEADS * width, 2 * HEADS * width), BF16),
            ((n_induce, 2 * HEADS * width), F32),
            ((n_class * ROW_HEADS + width, width), BF16),
            ((2, n_class, width), F32),
        ],
        inducing, induce_query, column_kvo, cell_qkvo, class_tokens, class_query, row_kvo,
        name="prep",
    )

    flags = (is_context == 1).astype(BF16).reshape(2, n_rows // 2)
    flags = jnp.repeat(flags.T, width // 2, axis=1)
    by_feat = jnp.transpose(cells, (1, 0, 2)).reshape(n_dev, own_feat * n_rows, width)
    payload = jnp.concatenate(
        [by_feat, jnp.broadcast_to(flags[None], (n_dev,) + flags.shape)], axis=1
    )
    received = lax.all_to_all(payload, "row", split_axis=0, concat_axis=0, tiled=True)
    partial, mask_row = call(
        functools.partial(column_kernel, own_feat, n_rows),
        [((n_total, full + width), BF16), ((8, n_total), F32)],
        received, col_q, fold, fold_base, row_qv,
        scratch=[
            pltpu.VMEM((own_feat, n_class * ROW_HEADS, n_total), F32),
            pltpu.VMEM((own_feat, width, n_total), F32),
        ],
        name="column",
    )
    parts = lax.all_to_all(
        partial.reshape(n_dev * n_split, local_rows, full + width),
        ("row", "feat"), split_axis=0, concat_axis=0, tiled=True,
    )
    own_flags = lax.dynamic_slice_in_dim(
        is_context, lax.axis_index("feat") * local_rows, local_rows
    ).reshape(1, local_rows)
    embed, icl_in, turned_query = call(
        row_kernel,
        [
            ((local_rows, full), BF16),
            ((local_rows, full), BF16),
            ((HEADS * local_rows, full), BF16),
        ],
        parts, own_flags, labels.reshape(1, local_rows), cls_sums, class_tokens, row_kvo[2],
        label_table, icl_query, icl_kvo,
        name="row",
    )
    rows = lax.all_gather(icl_in, ("row", "feat"), axis=0, tiled=True)
    (out,) = call(
        icl_kernel,
        [((local_rows, full), BF16)],
        rows, turned_query, mask_row, embed, icl_kvo,
        name="icl",
    )
    return out


def solution(mesh):
    return jax.shard_map(
        on_device,
        mesh=mesh,
        in_specs=(
            P(("group", "row"), "feat", None),
            P(("group", "row")),
            P(("group", "row", "feat")),
            P(), P(), P(), P(), P(), P(), P(), P(), P(), P(),
        ),
        out_specs=P(("group", "row", "feat"), None),
        check_vma=False,
    )
```

```python
import functools
import math

import jax
import jax.numpy as jnp
from jax import lax
from jax.experimental import pallas as pl
from jax.experimental.pallas import tpu as pltpu
from jax.sharding import PartitionSpec as P

HEADS = 4
ROW_HEADS = 8
EPSILON = 1e-06
LOG2E = math.log2(math.e)
F32 = jnp.float32
BF16 = jnp.bfloat16
NT = (((1,), (1,)), ((), ()))
TN = (((0,), (0,)), ((), ()))


def dot(a, b):
    return jnp.dot(a, b, preferred_element_type=F32)


def dot_nt(a, b):
    return lax.dot_general(a, b, NT, preferred_element_type=F32)


def head_rows(x, heads):
    width = x.shape[-1]
    lane = lax.broadcasted_iota(jnp.int32, x.shape, 1) // (width // heads)
    x = x.astype(F32)
    return jnp.concatenate(
        [jnp.where(lane == h, x, 0.0) for h in range(heads)], axis=0
    ).astype(BF16)


def prep_kernel(
    inducing,
    induce_query,
    column_kvo,
    cell_qkvo,
    class_tokens,
    class_query,
    row_kvo,
    col_q,
    fold,
    fold_base,
    row_qv,
    cls_sums,
):
    n_induce, width = inducing.shape
    scale = LOG2E / math.sqrt(width // HEADS)
    row_scale = LOG2E / math.sqrt(width // ROW_HEADS)
    iq = dot(inducing[...], induce_query[...]).astype(BF16)
    col_q[...] = (dot_nt(head_rows(iq, HEADS), column_kvo[0]) * scale).astype(BF16)
    mixed = dot(head_rows(column_kvo[1], HEADS), column_kvo[2]).astype(BF16)
    both = jnp.concatenate([mixed, inducing[...]], axis=0)
    keys = dot(both, cell_qkvo[1])
    values = dot(both, cell_qkvo[2])
    n_mixed = mixed.shape[0]
    n_both = n_mixed + n_induce
    g = dot_nt(head_rows(keys, HEADS), cell_qkvo[0]) * scale
    o = dot(head_rows(values, HEADS), cell_qkvo[3])
    for h in range(HEADS):
        for part, at in ((g, 0), (o, HEADS * width)):
            block = part[h * n_both : (h + 1) * n_both]
            lanes = slice(at + h * width, at + (h + 1) * width)
            fold[:, lanes] = block[:n_mixed].astype(BF16)
            fold_base[:, lanes] = block[n_mixed:]
    n_class = class_tokens.shape[0]
    tokens = class_tokens[...]
    rq = dot(tokens, class_query[...]).astype(BF16)
    lane = lax.broadcasted_iota(jnp.int32, (ROW_HEADS, width), 1) // (width // ROW_HEADS)
    head = lax.broadcasted_iota(jnp.int32, (ROW_HEADS, width), 0)
    rq32 = rq.astype(F32)
    blocks = jnp.concatenate(
        [jnp.where(lane == head, rq32[c : c + 1], 0.0) for c in range(n_class)], axis=0
    ).astype(BF16)
    row_qv[: n_class * ROW_HEADS] = (dot_nt(blocks, row_kvo[0]) * row_scale).astype(BF16)
    row_qv[n_class * ROW_HEADS :] = row_kvo[1].astype(F32).T.astype(BF16)
    ck = dot(tokens, row_kvo[0]).astype(BF16).astype(F32)
    cv = dot(tokens, row_kvo[1]).astype(BF16).astype(F32)
    same = (
        lax.broadcasted_iota(jnp.int32, (width, width), 0) // (width // ROW_HEADS)
        == lax.broadcasted_iota(jnp.int32, (width, width), 1) // (width // ROW_HEADS)
    ).astype(F32)
    numer = jnp.zeros((n_class, width), F32)
    denom = jnp.zeros((n_class, width), F32)
    for k in range(n_class):
        score = jnp.dot(
            rq32 * ck[k : k + 1], same, precision=lax.Precision.HIGHEST, preferred_element_type=F32
        )
        weight = jnp.exp2(score * row_scale)
        numer = numer + weight * cv[k : k + 1]
        denom = denom + weight
    cls_sums[0] = numer
    cls_sums[1] = denom


def pack_kernel(base, cells, flags, keep, send):
    n_rows = cells.shape[0]
    block = pltpu.einshape("rfw->frw", cells[...])
    out = block.reshape(-1, cells.shape[2])
    head = flags.shape[0]

    @pl.when(pl.program_id(0) % 2 == 0)
    def _():
        keep[0, :head] = flags[...]
        keep[0, head:] = out

    @pl.when(pl.program_id(0) % 2 == 1)
    def _():
        send[0, :head] = flags[...]
        send[0, head:] = out


def column_kernel(n_sources, n_feat, n_rows, head, first, last, *refs):
    sources, refs = refs[:n_sources], refs[n_sources:]
    if not first:
        before, refs = refs[0], refs[1:]
    col_q, fold, fold_base, row_qv, mask_ref, out, w_store, v_store = refs
    width = mask_ref.shape[1]
    n_total = mask_ref.shape[0]
    n_induce = fold_base.shape[0]
    n_weights = row_qv.shape[0] - width
    n_class = n_weights // ROW_HEADS
    full = n_class * width
    head_width = width // ROW_HEADS

    def feature(f, carry):
        cut = pl.ds(pl.multiple_of(head + f * n_rows, n_rows // 2), n_rows)
        x = jnp.concatenate(
            [s[:, part, cut, :].reshape(-1, width) for part in range(sources[0].shape[1]) for s in sources],
            axis=0,
        )
        xt = x.astype(F32).T
        xt_half = xt.astype(BF16)
        mask = mask_ref[...]
        p = jnp.exp2(dot(col_q[...], xt_half)).astype(BF16)
        sums = dot(p, jnp.concatenate([x * mask, mask], axis=1))
        y = (sums[:, :width] / sums[:, width:]).astype(BF16)
        y = jnp.concatenate(
            [y[h * n_induce : (h + 1) * n_induce] for h in range(HEADS)], axis=1
        )
        both = dot(y, fold[...]) + fold_base[...]
        g = jnp.concatenate([both[:, h * width : (h + 1) * width] for h in range(HEADS)], axis=0)
        o = jnp.concatenate(
            [both[:, h * width : (h + 1) * width] for h in range(HEADS, 2 * HEADS)], axis=0
        )
        s = jnp.exp2(dot(g.astype(BF16), xt_half))
        weights = []
        for h in range(HEADS):
            part = s[h * n_induce : (h + 1) * n_induce]
            weights.append((part * (1.0 / jnp.sum(part, axis=0, keepdims=True))).astype(BF16))
        res = xt + dot(o.T.astype(BF16), jnp.concatenate(weights, axis=0))
        mean = jnp.sum(res * res, axis=0, keepdims=True) * (1.0 / width)
        e = (res * lax.rsqrt(mean + EPSILON)).astype(BF16)
        wv = dot(row_qv[...], e)
        w_store[f] = jnp.exp2(wv[:n_weights])
        v_store[f] = wv[n_weights:]
        return carry

    lax.fori_loop(0, n_feat, feature, 0)

    step = min(n_total, 512)
    for at in range(0, n_total, step):
        lanes = slice(at, at + step)
        denom = w_store[0, :, lanes]
        for f in range(1, n_feat):
            denom = denom + w_store[f, :, lanes]
        if not first:
            denom = denom + before[full:, lanes]
        blocks = [[None] * ROW_HEADS for _ in range(n_class)]
        for h in range(ROW_HEADS):

            def add(f, acc):
                v = v_store[f, h * head_width : (h + 1) * head_width, lanes]
                return tuple(
                    acc[c] + w_store[f, pl.ds(c * ROW_HEADS + h, 1), lanes] * v
                    for c in range(n_class)
                )

            begin = [c * width + h * head_width for c in range(n_class)]
            if first:
                acc = (jnp.zeros((head_width, step), F32),) * n_class
            else:
                acc = tuple(before[b : b + head_width, lanes] for b in begin)
            acc = lax.fori_loop(0, n_feat, add, acc)
            for c in range(n_class):
                if last:
                    blocks[c][h] = acc[c]
                else:
                    out[begin[c] : begin[c] + head_width, lanes] = acc[c]
        if not last:
            out[full:, lanes] = denom
            continue
        for c in range(n_class):
            out[lanes, c * width : (c + 1) * width] = (
                jnp.concatenate(blocks[c], axis=0).T.astype(BF16)
            )
        padded = jnp.concatenate([denom, jnp.zeros((width - n_weights, step), F32)], axis=0)
        out[lanes, full:] = padded.T.astype(BF16)


def mask_kernel(n_sources, head, *refs):
    sources, (mask_out, mask_row) = refs[:n_sources], refs[n_sources:]
    width = mask_out.shape[1]
    flags = jnp.concatenate(
        [s[:, part, :head, :] for part in range(sources[0].shape[1]) for s in sources], axis=0
    ).astype(F32)
    lane = lax.broadcasted_iota(jnp.int32, flags.shape, 2)
    low = lane < width // 2
    turned = pltpu.roll(flags.reshape(-1, width), width // 2, 1).reshape(flags.shape)
    mask = jnp.concatenate(
        [jnp.where(low, flags, turned), jnp.where(low, turned, flags)], axis=1
    ).reshape(mask_out.shape)
    mask_row[...] = mask.T[: mask_row.shape[0]]
    mask_out[...] = (mask * 0.125).astype(BF16)


def row_kernel(
    paired, own, other, flags, labels, cls_sums, class_tokens, row_out, table, embed, icl_in
):
    n_class, width = class_tokens.shape
    full = n_class * width
    if paired:
        total = jnp.concatenate(
            [own[p].astype(F32) + other[1 - p].astype(F32) for p in range(2)], axis=0
        )
    else:
        total = jnp.sum(own[...].astype(F32), axis=0)
    lane = lax.broadcasted_iota(jnp.int32, (width, full), 1) // (width // ROW_HEADS)
    spread = (lax.broadcasted_iota(jnp.int32, (width, full), 0) == lane).astype(F32)
    denom = jnp.dot(
        total[:, full:], spread, precision=lax.Precision.HIGHEST, preferred_element_type=F32
    )
    pieces = []
    for c in range(n_class):
        lanes = slice(c * width, (c + 1) * width)
        mix = (total[:, lanes] + cls_sums[0, c : c + 1]) / (
            denom[:, lanes] + cls_sums[1, c : c + 1]
        )
        pieces.append(
            class_tokens[c : c + 1].astype(F32) + dot(mix.astype(BF16), row_out[2])
        )
    row_embed = jnp.concatenate(pieces, axis=1).astype(BF16)
    embed[...] = row_embed[: embed.shape[0]]
    classes = table.shape[0]
    hot = lax.broadcasted_iota(jnp.int32, (classes, labels.shape[1]), 0) == labels[...]
    hot = jnp.where(hot & (flags[...] == 1), 1.0, 0.0).astype(F32)
    label = lax.dot_general(hot, table[...].astype(F32), TN, preferred_element_type=F32)
    icl_in[...] = (row_embed.astype(F32) + label).astype(BF16)


def query_kernel(embed, icl_query, icl_kvo, turned_query):
    n_rows, full = embed.shape
    query = dot(embed[...], icl_query[...]).astype(BF16)
    head = full // HEADS
    scale = LOG2E / math.sqrt(head)
    for h in range(HEADS):
        lanes = slice(h * head, (h + 1) * head)
        turned_query[h * n_rows : (h + 1) * n_rows] = (
            dot_nt(query[:, lanes], icl_kvo[0, :, lanes]) * scale
        ).astype(BF16)


def icl_kernel(n_parts, *refs):
    parts, (turned_query, mask_row, embed, icl_kvo, out) = refs[:n_parts], refs[n_parts:]
    rows = jnp.concatenate([r[...] for r in parts], axis=0)
    full = rows.shape[1]
    n_rows = embed.shape[0]
    head = full // HEADS
    s = dot_nt(turned_query[...], rows)
    s = jnp.where(mask_row[0:1] > 0.5, s, -1e30)
    p = jnp.exp2(s - jnp.max(s, axis=1, keepdims=True))
    denom = jnp.sum(p, axis=1, keepdims=True)
    y = (dot(p.astype(BF16), rows) / denom).astype(BF16)
    mix = jnp.concatenate(
        [
            dot(y[h * n_rows : (h + 1) * n_rows], icl_kvo[1, :, h * head : (h + 1) * head])
            for h in range(HEADS)
        ],
        axis=1,
    ).astype(BF16)
    out[...] = (embed[...].astype(F32) + dot(mix, icl_kvo[2])).astype(BF16)


def call(kernel, outs, *args, scratch=(), mib=16, cost=None, name=None):
    return pl.pallas_call(
        kernel,
        out_shape=tuple(jax.ShapeDtypeStruct(s, d) for s, d in outs),
        in_specs=[pl.BlockSpec(memory_space=pltpu.VMEM)] * len(args),
        out_specs=tuple(pl.BlockSpec(memory_space=pltpu.VMEM) for _ in outs),
        scratch_shapes=scratch,
        compiler_params=pltpu.CompilerParams(vmem_limit_bytes=mib * 1024 * 1024),
        cost_estimate=cost,
        name=name,
    )(*args)


def swap(x, distance):
    n_dev = lax.axis_size("row")
    return lax.ppermute(x, "row", [(s, s ^ distance) for s in range(n_dev)])


CHUNKS = (8, 8)


def on_device(
    cells,
    is_context,
    labels,
    inducing,
    induce_query,
    column_kvo,
    cell_qkvo,
    class_tokens,
    class_query,
    row_kvo,
    label_table,
    icl_query,
    icl_kvo,
):
    n_rows, n_feat, width = cells.shape
    n_induce = inducing.shape[0]
    n_class = class_tokens.shape[0]
    n_dev = lax.axis_size("row")
    n_split = lax.axis_size("feat")
    own_feat = n_feat // n_dev
    n_total = n_dev * n_rows
    local_rows = n_rows // n_split
    full = n_class * width
    n_weights = n_class * ROW_HEADS
    paired = n_split == 1 and n_dev == 16

    prepared = call(
        prep_kernel,
        [
            ((HEADS * n_induce, width), BF16),
            ((HEADS * width, 2 * HEADS * width), BF16),
            ((n_induce, 2 * HEADS * width), F32),
            ((n_weights + width, width), BF16),
            ((2, n_class, width), F32),
        ],
        inducing, induce_query, column_kvo, cell_qkvo, class_tokens, class_query, row_kvo,
        name="prep",
    )
    folded, cls_sums = prepared[:4], prepared[4]

    flags = (is_context == 1).astype(BF16).reshape(2, n_rows // 2)
    flags = jnp.repeat(flags.T, width // 2, axis=1)
    head = n_rows // 2
    size = head + own_feat * n_rows

    chunks = CHUNKS if paired and sum(CHUNKS) == own_feat else (own_feat,)
    chips = n_dev // 2
    groups = []
    if paired:
        me = lax.axis_index("row").astype(jnp.int32).reshape(1)
        shape = jax.ShapeDtypeStruct((chips, size, width), BF16)
        spec = pl.BlockSpec((1, size, width), lambda k, base: (k // 2, 0, 0))
        keep, send = pl.pallas_call(
            pack_kernel,
            grid_spec=pltpu.PrefetchScalarGridSpec(
                num_scalar_prefetch=1,
                grid=(n_dev,),
                in_specs=[
                    pl.BlockSpec((n_rows, own_feat, width), lambda k, base: (0, base[0] ^ k, 0)),
                    pl.BlockSpec(flags.shape, lambda k, base: (0, 0)),
                ],
                out_specs=(spec, spec),
            ),
            out_shape=(shape, shape),
            compiler_params=pltpu.CompilerParams(vmem_limit_bytes=16 * 1024 * 1024),
            name="pack",
        )(me, cells, flags)
        at = 0
        for c, n in enumerate(chunks):
            end = at + n * n_rows + (head if c == 0 else 0)
            got = swap(send[:, at:end], 1)
            both = jnp.stack([keep[:, at:end], got], axis=1)
            group = {0: both[:1]}
            for q in (4, 6, 5, 7, 2, 3, 1):
                group[q] = swap(both[q : q + 1], 2 * q)
            groups.append([group[q] for q in range(chips)])
            at = end
    else:
        by_feat = jnp.transpose(cells, (1, 0, 2)).reshape(n_dev, own_feat * n_rows, width)
        payload = jnp.concatenate(
            [jnp.broadcast_to(flags[None], (n_dev,) + flags.shape), by_feat], axis=1
        )
        got = lax.all_to_all(payload, "row", split_axis=0, concat_axis=0, tiled=True)
        groups.append([got[:, None]])

    mask, mask_row = call(
        functools.partial(mask_kernel, len(groups[0]), head),
        [((n_total, width), BF16), ((8, n_total), F32)],
        *groups[0],
        name="mask",
    )
    state = ()
    for c, n in enumerate(chunks):
        last = c == len(chunks) - 1
        state = call(
            functools.partial(
                column_kernel, len(groups[c]), n, n_rows, 0 if c else head, c == 0, last
            ),
            [((n_total, full + width), BF16) if last else ((full + n_weights, n_total), F32)],
            *groups[c], *state, *folded, mask,
            scratch=[
                pltpu.VMEM((n, n_weights, n_total), F32),
                pltpu.VMEM((n, width, n_total), F32),
            ],
            mib=24,
            cost=pl.CostEstimate(
                flops=n * n_total * width * 4000, transcendentals=0, bytes_accessed=4 * 1024 * 1024
            ),
            name="column",
        )
    (partial,) = state

    if paired:
        half = partial.reshape(2, chips, n_rows, full + width)
        got = swap(half[1], 1)
        sums = (half[0].astype(F32) + got.astype(F32)).astype(BF16)
        sums = sums.reshape(chips // 2, 2, n_rows, full + width)
        own = sums[0].astype(F32)
        for z in (2, 3, 1):
            own = own + swap(sums[z], 4 * z).astype(F32)
        own = own.astype(BF16)
        other = swap(own, 2)
        ids = jnp.stack([is_context, labels])
        ids = jnp.concatenate([ids, swap(ids, 2)], axis=1)
        own_flags, own_labels = ids[:1], ids[1:]
    else:
        own = lax.all_to_all(
            partial.reshape(n_dev * n_split, local_rows, full + width),
            ("row", "feat"), split_axis=0, concat_axis=0, tiled=True,
        )
        other = cls_sums
        own_flags = lax.dynamic_slice_in_dim(
            is_context, lax.axis_index("feat") * local_rows, local_rows
        ).reshape(1, local_rows)
        own_labels = labels.reshape(1, local_rows)
    embed, icl_in = call(
        functools.partial(row_kernel, paired),
        [((local_rows, full), BF16), ((own_labels.shape[1], full), BF16)],
        own, other, own_flags, own_labels, cls_sums, class_tokens, row_kvo, label_table,
        name="row",
    )
    if paired:
        near = jnp.concatenate([icl_in] + [swap(icl_in, 4 * z) for z in range(1, chips // 2)])
        rows = (near, swap(near, 1))
    else:
        rows = (lax.all_gather(icl_in, ("row", "feat"), axis=0, tiled=True),)
    (turned_query,) = call(
        query_kernel,
        [((HEADS * local_rows, full), BF16)],
        embed, icl_query, icl_kvo,
        name="query",
    )
    (out,) = call(
        functools.partial(icl_kernel, len(rows)),
        [((local_rows, full), BF16)],
        *rows, turned_query, mask_row, embed, icl_kvo,
        name="icl",
    )
    return out


def solution(mesh):
    return jax.shard_map(
        on_device,
        mesh=mesh,
        in_specs=(
            P(("group", "row"), "feat", None),
            P(("group", "row")),
            P(("group", "row", "feat")),
            P(), P(), P(), P(), P(), P(), P(), P(), P(), P(),
        ),
        out_specs=P(("group", "row", "feat"), None),
        check_vma=False,
    )
```

```python
import functools
import math

import jax
import jax.numpy as jnp
from jax import lax
from jax.experimental import pallas as pl
from jax.experimental.pallas import tpu as pltpu
from jax.sharding import PartitionSpec as P

HEADS = 4
ROW_HEADS = 8
EPSILON = 1e-06
LOG2E = math.log2(math.e)
F32 = jnp.float32
BF16 = jnp.bfloat16
NT = (((1,), (1,)), ((), ()))
TN = (((0,), (0,)), ((), ()))


def dot(a, b):
    return jnp.dot(a, b, preferred_element_type=F32)


def dot_nt(a, b):
    return lax.dot_general(a, b, NT, preferred_element_type=F32)


def head_rows(x, heads):
    width = x.shape[-1]
    lane = lax.broadcasted_iota(jnp.int32, x.shape, 1) // (width // heads)
    x = x.astype(F32)
    return jnp.concatenate(
        [jnp.where(lane == h, x, 0.0) for h in range(heads)], axis=0
    ).astype(BF16)


def prep_kernel(
    inducing,
    induce_query,
    column_kvo,
    cell_qkvo,
    class_tokens,
    class_query,
    row_kvo,
    col_q,
    fold,
    fold_base,
    row_qv,
    cls_sums,
):
    n_induce, width = inducing.shape
    scale = LOG2E / math.sqrt(width // HEADS)
    row_scale = LOG2E / math.sqrt(width // ROW_HEADS)
    iq = dot(inducing[...], induce_query[...]).astype(BF16)
    col_q[...] = (dot_nt(head_rows(iq, HEADS), column_kvo[0]) * scale).astype(BF16)
    mixed = dot(head_rows(column_kvo[1], HEADS), column_kvo[2]).astype(BF16)
    both = jnp.concatenate([mixed, inducing[...]], axis=0)
    keys = dot(both, cell_qkvo[1])
    values = dot(both, cell_qkvo[2])
    n_mixed = mixed.shape[0]
    n_both = n_mixed + n_induce
    g = dot_nt(head_rows(keys, HEADS), cell_qkvo[0]) * scale
    o = dot(head_rows(values, HEADS), cell_qkvo[3])
    for h in range(HEADS):
        for part, at in ((g, 0), (o, HEADS * width)):
            block = part[h * n_both : (h + 1) * n_both]
            lanes = slice(at + h * width, at + (h + 1) * width)
            fold[:, lanes] = block[:n_mixed].astype(BF16)
            fold_base[:, lanes] = block[n_mixed:]
    n_class = class_tokens.shape[0]
    tokens = class_tokens[...]
    rq = dot(tokens, class_query[...]).astype(BF16)
    lane = lax.broadcasted_iota(jnp.int32, (ROW_HEADS, width), 1) // (width // ROW_HEADS)
    head = lax.broadcasted_iota(jnp.int32, (ROW_HEADS, width), 0)
    rq32 = rq.astype(F32)
    blocks = jnp.concatenate(
        [jnp.where(lane == head, rq32[c : c + 1], 0.0) for c in range(n_class)], axis=0
    ).astype(BF16)
    row_qv[: n_class * ROW_HEADS] = (dot_nt(blocks, row_kvo[0]) * row_scale).astype(BF16)
    row_qv[n_class * ROW_HEADS :] = row_kvo[1].astype(F32).T.astype(BF16)
    ck = dot(tokens, row_kvo[0]).astype(BF16).astype(F32)
    cv = dot(tokens, row_kvo[1]).astype(BF16).astype(F32)
    same = (
        lax.broadcasted_iota(jnp.int32, (width, width), 0) // (width // ROW_HEADS)
        == lax.broadcasted_iota(jnp.int32, (width, width), 1) // (width // ROW_HEADS)
    ).astype(F32)
    numer = jnp.zeros((n_class, width), F32)
    denom = jnp.zeros((n_class, width), F32)
    for k in range(n_class):
        score = jnp.dot(
            rq32 * ck[k : k + 1], same, precision=lax.Precision.HIGHEST, preferred_element_type=F32
        )
        weight = jnp.exp2(score * row_scale)
        numer = numer + weight * cv[k : k + 1]
        denom = denom + weight
    cls_sums[0] = numer
    cls_sums[1] = denom


def notes_tile(flags, labels, width):
    n_rows = flags.shape[1]
    half = n_rows // 2
    same = lax.broadcasted_iota(jnp.int32, (n_rows, n_rows), 0) == lax.broadcasted_iota(
        jnp.int32, (n_rows, n_rows), 1
    )

    def column(row):
        return jnp.sum(jnp.where(same, row, 0.0), axis=1, keepdims=True)

    flag = column(jnp.where(flags == 1, 1.0, 0.0))
    label = column(labels.astype(F32))
    quarter = lax.broadcasted_iota(jnp.int32, (half, width), 1) // (width // 4)
    tile = jnp.where(quarter == 0, flag[:half], label[:half])
    tile = jnp.where(quarter == 2, flag[half:], tile)
    return jnp.where(quarter == 3, label[half:], tile).astype(BF16)


def pack_kernel(axis, feats, n_own, start, head, cells, flags, labels, keep, send, block, sem):
    n_dev = block.shape[0]
    n_rows, width = cells.shape[0], cells.shape[2]
    me = lax.axis_index(axis)
    copies = []
    for k in range(n_dev):
        at = pl.multiple_of((me ^ k) * n_own + start, math.gcd(n_own, start))
        copies.append(
            pltpu.make_async_copy(cells.at[:, pl.ds(at, feats), :], block.at[k], sem.at[k])
        )
    order = [k for k in range(n_dev) if k % 2] + [k for k in range(n_dev) if k % 2 == 0]
    for k in order:
        copies[k].start()
    if head:
        tile = notes_tile(flags[...], labels[...], width)
    for k in order:
        copies[k].wait()
        out = (keep, send)[k % 2]
        if head:
            out[k // 2, :head] = tile
        out[k // 2, head:] = pltpu.einshape("rfw->frw", block[k]).reshape(-1, width)


def sum_kernel(*refs):
    parts, out = refs[:-1], refs[-1]
    total = parts[0][...].astype(F32)
    for p in parts[1:]:
        total = total + p[...].astype(F32)
    out[...] = total.astype(out.dtype)


def sort_refs(refs, order):
    return [refs[order.index(i)] for i in range(len(order))], refs[len(order) :]


def in_groups(count, step, body):
    step = math.gcd(count, step)
    if step == count:
        for i in range(count):
            body(i)
        return

    def turn(t, carry):
        for i in range(step):
            body(t * step + i)
        return carry

    lax.fori_loop(0, count // step, turn, 0)


def column_kernel(order, n_feat, n_rows, head, first, last, *refs):
    sources, refs = sort_refs(refs, order)
    if not first:
        before, refs = refs[0], refs[1:]
    col_q, fold, fold_base, row_qv, mask_ref, out, xt_store, y_store, g_store, w_store, v_store = refs
    width = mask_ref.shape[1]
    n_total = mask_ref.shape[0]
    n_induce = fold_base.shape[0]
    n_weights = row_qv.shape[0] - width
    n_class = n_weights // ROW_HEADS
    full = n_class * width
    head_width = width // ROW_HEADS

    def induce(f):
        cut = pl.ds(pl.multiple_of(head + f * n_rows, n_rows // 2), n_rows)
        x = jnp.concatenate(
            [
                s[:, part, cut, :].reshape(-1, width)
                for part in range(sources[0].shape[1])
                for s in sources
            ],
            axis=0,
        )
        xt = x.T
        xt_store[f] = xt
        mask = mask_ref[...]
        p = jnp.exp2(dot(col_q[...], xt)).astype(BF16)
        sums = dot(p, jnp.concatenate([x * mask, mask], axis=1))
        y = (sums[:, :width] / sums[:, width:]).astype(BF16)
        rows = pl.ds(pl.multiple_of(f * n_induce, n_induce), n_induce)
        for h in range(HEADS):
            y_store[rows, h * width : (h + 1) * width] = y[h * n_induce : (h + 1) * n_induce]

    in_groups(n_feat, 8, induce)

    for j in range(HEADS):
        lanes = slice(2 * j * width, (2 * j + 2) * width)
        both = dot(y_store[...], fold[:, lanes])
        for f in range(n_feat):
            part = (both[f * n_induce : (f + 1) * n_induce] + fold_base[:, lanes]).astype(BF16)
            for i in range(2):
                h = 2 * j + i
                g_store[f, h * n_induce : (h + 1) * n_induce] = part[:, i * width : (i + 1) * width]

    def attend(f):
        g = g_store[f, : HEADS * n_induce]
        o = g_store[f, HEADS * n_induce :]
        xt = xt_store[f]
        s = jnp.exp2(dot(g, xt))
        weights = []
        for h in range(HEADS):
            part = s[h * n_induce : (h + 1) * n_induce]
            weights.append((part * (1.0 / jnp.sum(part, axis=0, keepdims=True))).astype(BF16))
        res = xt.astype(F32) + dot(o.T, jnp.concatenate(weights, axis=0))
        mean = jnp.sum(res * res, axis=0, keepdims=True) * (1.0 / width)
        e = (res * lax.rsqrt(mean + EPSILON)).astype(BF16)
        wv = dot(row_qv[...], e)
        w_store[f] = jnp.exp2(wv[:n_weights])
        v_store[f] = wv[n_weights:]

    in_groups(n_feat, 8, attend)

    step = min(n_total, 512)
    for at in range(0, n_total, step):
        lanes = slice(at, at + step)
        denom = w_store[0, :, lanes]
        for f in range(1, n_feat):
            denom = denom + w_store[f, :, lanes]
        if not first:
            denom = denom + before[full:, lanes]
        blocks = [[None] * ROW_HEADS for _ in range(n_class)]
        for h in range(ROW_HEADS):
            begin = [c * width + h * head_width for c in range(n_class)]
            acc = [None if first else before[b : b + head_width, lanes] for b in begin]
            for f in range(n_feat):
                v = v_store[f, h * head_width : (h + 1) * head_width, lanes]
                for c in range(n_class):
                    term = w_store[f, pl.ds(c * ROW_HEADS + h, 1), lanes] * v
                    acc[c] = term if acc[c] is None else acc[c] + term
            for c in range(n_class):
                if last:
                    blocks[c][h] = acc[c].astype(BF16)
                else:
                    out[begin[c] : begin[c] + head_width, lanes] = acc[c]
        if not last:
            out[full:, lanes] = denom
            continue
        for c in range(n_class):
            out[lanes, c * width : (c + 1) * width] = jnp.concatenate(blocks[c], axis=0).T
        padded = jnp.concatenate([denom, jnp.zeros((width - n_weights, step), F32)], axis=0)
        out[lanes, full:] = padded.astype(BF16).T


def notes_kernel(order, head, *refs):
    sources, (mask_out, mask_row, label_row) = sort_refs(refs, order)
    width = mask_out.shape[1]
    tile = jnp.concatenate(
        [s[:, part, :head, :] for part in range(sources[0].shape[1]) for s in sources], axis=0
    ).astype(F32)

    def spread(quarter):
        pieces = [
            jnp.broadcast_to(tile[:, :, q * (width // 4) : q * (width // 4) + 1], tile.shape)
            for q in (quarter, quarter + 2)
        ]
        return jnp.concatenate(pieces, axis=1).reshape(mask_out.shape)

    mask = spread(0)
    mask_out[...] = (mask * 0.125).astype(BF16)
    mask_row[...] = mask.T[: mask_row.shape[0]]
    label_row[...] = spread(1).T[: label_row.shape[0]]


def row_kernel(
    paired, own, other, flags, labels, cls_sums, class_tokens, row_out, table, embed, icl_in
):
    n_class, width = class_tokens.shape
    full = n_class * width
    if paired:
        total = jnp.concatenate(
            [own[p].astype(F32) + other[1 - p].astype(F32) for p in range(2)], axis=0
        )
    else:
        total = jnp.sum(own[...].astype(F32), axis=0)
    lane = lax.broadcasted_iota(jnp.int32, (width, full), 1) // (width // ROW_HEADS)
    spread = (lax.broadcasted_iota(jnp.int32, (width, full), 0) == lane).astype(F32)
    denom = jnp.dot(
        total[:, full:], spread, precision=lax.Precision.HIGHEST, preferred_element_type=F32
    )
    pieces = []
    for c in range(n_class):
        lanes = slice(c * width, (c + 1) * width)
        mix = (total[:, lanes] + cls_sums[0, c : c + 1]) / (
            denom[:, lanes] + cls_sums[1, c : c + 1]
        )
        pieces.append(
            class_tokens[c : c + 1].astype(F32) + dot(mix.astype(BF16), row_out[2])
        )
    row_embed = jnp.concatenate(pieces, axis=1).astype(BF16)
    embed[...] = row_embed[: embed.shape[0]]
    classes, n_rows = table.shape[0], icl_in.shape[0]
    number = lax.broadcasted_iota(jnp.int32, (classes, n_rows), 0).astype(F32)
    hot = number == labels[0:1, :n_rows].astype(F32)
    hot = jnp.where(hot & (flags[0:1, :n_rows].astype(F32) == 1.0), 1.0, 0.0).astype(F32)
    label = lax.dot_general(hot, table[...].astype(F32), TN, preferred_element_type=F32)
    icl_in[...] = (row_embed.astype(F32) + label).astype(BF16)


def query_kernel(embed, icl_query, icl_kvo, turned_query):
    n_rows, full = embed.shape
    query = dot(embed[...], icl_query[...]).astype(BF16)
    head = full // HEADS
    scale = LOG2E / math.sqrt(head)
    for h in range(HEADS):
        lanes = slice(h * head, (h + 1) * head)
        turned_query[h * n_rows : (h + 1) * n_rows] = (
            dot_nt(query[:, lanes], icl_kvo[0, :, lanes]) * scale
        ).astype(BF16)


def icl_kernel(order, *refs):
    parts, (turned_query, mask_row, embed, icl_kvo, out) = sort_refs(refs, order)
    rows = jnp.concatenate([r[...] for r in parts], axis=0)
    full = rows.shape[1]
    n_rows = embed.shape[0]
    head = full // HEADS
    s = dot_nt(turned_query[...], rows)
    s = jnp.where(mask_row[0:1] > 0.5, s, -1e30)
    p = jnp.exp2(s - jnp.max(s, axis=1, keepdims=True))
    denom = jnp.sum(p, axis=1, keepdims=True)
    y = (dot(p.astype(BF16), rows) / denom).astype(BF16)
    mix = jnp.concatenate(
        [
            dot(y[h * n_rows : (h + 1) * n_rows], icl_kvo[1, :, h * head : (h + 1) * head])
            for h in range(HEADS)
        ],
        axis=1,
    ).astype(BF16)
    out[...] = (embed[...].astype(F32) + dot(mix, icl_kvo[2])).astype(BF16)


def call(kernel, outs, *args, scratch=(), mib=16, cost=None, name=None):
    return pl.pallas_call(
        kernel,
        out_shape=tuple(jax.ShapeDtypeStruct(s, d) for s, d in outs),
        in_specs=[pl.BlockSpec(memory_space=pltpu.VMEM)] * len(args),
        out_specs=tuple(pl.BlockSpec(memory_space=pltpu.VMEM) for _ in outs),
        scratch_shapes=scratch,
        compiler_params=pltpu.CompilerParams(vmem_limit_bytes=mib * 1024 * 1024),
        cost_estimate=cost,
        name=name,
    )(*args)


def swap(x, distance):
    n_dev = lax.axis_size("row")
    return lax.ppermute(x, "row", [(s, s ^ distance) for s in range(n_dev)])


CHUNKS = (8, 8)
ORDER = (6, 7, 4, 5, 2, 3, 1)
Z_ORDER = (3, 2, 1)


def on_device(
    cells,
    is_context,
    labels,
    inducing,
    induce_query,
    column_kvo,
    cell_qkvo,
    class_tokens,
    class_query,
    row_kvo,
    label_table,
    icl_query,
    icl_kvo,
):
    n_rows, n_feat, width = cells.shape
    n_induce = inducing.shape[0]
    n_class = class_tokens.shape[0]
    n_dev = lax.axis_size("row")
    n_split = lax.axis_size("feat")
    own_feat = n_feat // n_dev
    n_total = n_dev * n_rows
    local_rows = n_rows // n_split
    full = n_class * width
    n_weights = n_class * ROW_HEADS
    paired = n_split == 1 and n_dev == 16

    prepared = call(
        prep_kernel,
        [
            ((HEADS * n_induce, width), BF16),
            ((HEADS * width, 2 * HEADS * width), BF16),
            ((n_induce, 2 * HEADS * width), F32),
            ((n_weights + width, width), BF16),
            ((2, n_class, width), F32),
        ],
        inducing, induce_query, column_kvo, cell_qkvo, class_tokens, class_query, row_kvo,
        name="prep",
    )
    folded, cls_sums = prepared[:4], prepared[4]

    head = n_rows // 2
    chunks = CHUNKS if paired and sum(CHUNKS) == own_feat else (own_feat,)
    chips = n_dev // 2
    groups = []
    if paired:
        order = (0,) + ORDER
        at = 0
        for c, n in enumerate(chunks):
            top = 0 if c else head
            keep, send = pl.pallas_call(
                functools.partial(pack_kernel, "row", n, own_feat, at, top),
                in_specs=[
                    pl.BlockSpec(memory_space=pltpu.MemorySpace.HBM),
                    pl.BlockSpec(memory_space=pltpu.VMEM),
                    pl.BlockSpec(memory_space=pltpu.VMEM),
                ],
                out_specs=(pl.BlockSpec(memory_space=pltpu.VMEM),) * 2,
                out_shape=(jax.ShapeDtypeStruct((chips, top + n * n_rows, width), BF16),) * 2,
                scratch_shapes=[
                    pltpu.VMEM((n_dev, n_rows, n, width), BF16),
                    pltpu.SemaphoreType.DMA((n_dev,)),
                ],
                compiler_params=pltpu.CompilerParams(vmem_limit_bytes=8 * 1024 * 1024),
                name="pack",
            )(cells, is_context.reshape(1, n_rows), labels.reshape(1, n_rows))
            got = swap(send, 1)
            both = jnp.stack([keep, got], axis=1)
            groups.append([both[:1]] + [swap(both[q : q + 1], 2 * q) for q in ORDER])
            at += n
    else:
        order = (0,)
        by_feat = jnp.transpose(cells, (1, 0, 2)).reshape(n_dev, own_feat * n_rows, width)
        flags = jnp.where(is_context == 1, 1.0, 0.0).astype(BF16).reshape(2, head)
        tile = jnp.repeat(flags.T, width // 2, axis=1)
        payload = jnp.concatenate(
            [jnp.broadcast_to(tile[None], (n_dev,) + tile.shape), by_feat], axis=1
        )
        got = lax.all_to_all(payload, "row", split_axis=0, concat_axis=0, tiled=True)
        groups.append([got[:, None]])

    mask, mask_row, label_row = call(
        functools.partial(notes_kernel, order, head),
        [((n_total, width), BF16), ((8, n_total), F32), ((8, n_total), F32)],
        *groups[0],
        name="notes",
    )
    state = ()
    for c, n in enumerate(chunks):
        last = c == len(chunks) - 1
        state = call(
            functools.partial(column_kernel, order, n, n_rows, 0 if c else head, c == 0, last),
            [((n_total, full + width), BF16) if last else ((full + n_weights, n_total), F32)],
            *groups[c], *state, *folded, mask,
            scratch=[
                pltpu.VMEM((n, width, n_total), BF16),
                pltpu.VMEM((n * n_induce, HEADS * width), BF16),
                pltpu.VMEM((n, 2 * HEADS * n_induce, width), BF16),
                pltpu.VMEM((n, n_weights, n_total), F32),
                pltpu.VMEM((n, width, n_total), F32),
            ],
            mib=24,
            cost=pl.CostEstimate(
                flops=n * n_total * width * 4000, transcendentals=0, bytes_accessed=4 * 1024 * 1024
            ),
            name="column",
        )
    (partial,) = state

    if paired:
        half = partial.reshape(2, chips, n_rows, full + width)
        (sums,) = call(
            sum_kernel, [(half.shape[1:], BF16)], half[0], swap(half[1], 1), name="sum"
        )
        sums = sums.reshape(chips // 2, 2, n_rows, full + width)
        (own,) = call(
            sum_kernel,
            [(sums.shape[1:], BF16)],
            sums[0], *[swap(sums[z], 4 * z) for z in Z_ORDER],
            name="sum",
        )
        other = swap(own, 2)
        own_flags, own_labels, near = mask_row, label_row, 2 * n_rows
    else:
        own = lax.all_to_all(
            partial.reshape(n_dev * n_split, local_rows, full + width),
            ("row", "feat"), split_axis=0, concat_axis=0, tiled=True,
        )
        other = cls_sums
        own_flags = lax.dynamic_slice_in_dim(
            is_context, lax.axis_index("feat") * local_rows, local_rows
        ).reshape(1, local_rows)
        own_labels, near = labels.reshape(1, local_rows), local_rows
    embed, icl_in = call(
        functools.partial(row_kernel, paired),
        [((local_rows, full), BF16), ((near, full), BF16)],
        own, other, own_flags, own_labels, cls_sums, class_tokens, row_kvo, label_table,
        name="row",
    )
    if paired:
        z_order = (0,) + Z_ORDER
        mine = [icl_in] + [swap(icl_in, 4 * z) for z in Z_ORDER]
        rows = mine + [swap(r, 1) for r in mine]
        row_order = z_order + tuple(chips // 2 + z for z in z_order)
    else:
        rows = (lax.all_gather(icl_in, ("row", "feat"), axis=0, tiled=True),)
        row_order = (0,)
    (turned_query,) = call(
        query_kernel,
        [((HEADS * local_rows, full), BF16)],
        embed, icl_query, icl_kvo,
        name="query",
    )
    (out,) = call(
        functools.partial(icl_kernel, row_order),
        [((local_rows, full), BF16)],
        *rows, turned_query, mask_row, embed, icl_kvo,
        name="icl",
    )
    return out


def solution(mesh):
    return jax.shard_map(
        on_device,
        mesh=mesh,
        in_specs=(
            P(("group", "row"), "feat", None),
            P(("group", "row")),
            P(("group", "row", "feat")),
            P(), P(), P(), P(), P(), P(), P(), P(), P(), P(),
        ),
        out_specs=P(("group", "row", "feat"), None),
        check_vma=False,
    )
```

```python
import functools
import math

import jax
import jax.numpy as jnp
from jax import lax
from jax.experimental import pallas as pl
from jax.experimental.pallas import tpu as pltpu
from jax.sharding import PartitionSpec as P

HEADS = 4
ROW_HEADS = 8
EPSILON = 1e-06
LOG2E = math.log2(math.e)
F32 = jnp.float32
BF16 = jnp.bfloat16
NT = (((1,), (1,)), ((), ()))
TN = (((0,), (0,)), ((), ()))


def dot(a, b):
    return jnp.dot(a, b, preferred_element_type=F32)


def dot_nt(a, b):
    return lax.dot_general(a, b, NT, preferred_element_type=F32)


def head_rows(x, heads):
    width = x.shape[-1]
    lane = lax.broadcasted_iota(jnp.int32, x.shape, 1) // (width // heads)
    x = x.astype(F32)
    return jnp.concatenate(
        [jnp.where(lane == h, x, 0.0) for h in range(heads)], axis=0
    ).astype(BF16)


def prep_kernel(
    inducing,
    induce_query,
    column_kvo,
    cell_qkvo,
    class_tokens,
    class_query,
    row_kvo,
    col_q,
    fold,
    fold_base,
    row_qv,
    cls_sums,
):
    n_induce, width = inducing.shape
    scale = LOG2E / math.sqrt(width // HEADS)
    row_scale = LOG2E / math.sqrt(width // ROW_HEADS)
    iq = dot(inducing[...], induce_query[...]).astype(BF16)
    col_q[...] = (dot_nt(head_rows(iq, HEADS), column_kvo[0]) * scale).astype(BF16)
    mixed = dot(head_rows(column_kvo[1], HEADS), column_kvo[2]).astype(BF16)
    both = jnp.concatenate([mixed, inducing[...]], axis=0)
    keys = dot(both, cell_qkvo[1])
    values = dot(both, cell_qkvo[2])
    n_mixed = mixed.shape[0]
    n_both = n_mixed + n_induce
    g = dot_nt(head_rows(keys, HEADS), cell_qkvo[0]) * scale
    o = dot(head_rows(values, HEADS), cell_qkvo[3])
    for h in range(HEADS):
        for part, at in ((g, 0), (o, HEADS * width)):
            block = part[h * n_both : (h + 1) * n_both]
            lanes = slice(at + h * width, at + (h + 1) * width)
            fold[:, lanes] = block[:n_mixed].astype(BF16)
            fold_base[:, lanes] = block[n_mixed:]
    n_class = class_tokens.shape[0]
    tokens = class_tokens[...]
    rq = dot(tokens, class_query[...]).astype(BF16)
    lane = lax.broadcasted_iota(jnp.int32, (ROW_HEADS, width), 1) // (width // ROW_HEADS)
    head = lax.broadcasted_iota(jnp.int32, (ROW_HEADS, width), 0)
    rq32 = rq.astype(F32)
    blocks = jnp.concatenate(
        [jnp.where(lane == head, rq32[c : c + 1], 0.0) for c in range(n_class)], axis=0
    ).astype(BF16)
    row_qv[: n_class * ROW_HEADS] = (dot_nt(blocks, row_kvo[0]) * row_scale).astype(BF16)
    row_qv[n_class * ROW_HEADS :] = row_kvo[1].astype(F32).T.astype(BF16)
    ck = dot(tokens, row_kvo[0]).astype(BF16).astype(F32)
    cv = dot(tokens, row_kvo[1]).astype(BF16).astype(F32)
    same = (
        lax.broadcasted_iota(jnp.int32, (width, width), 0) // (width // ROW_HEADS)
        == lax.broadcasted_iota(jnp.int32, (width, width), 1) // (width // ROW_HEADS)
    ).astype(F32)
    numer = jnp.zeros((n_class, width), F32)
    denom = jnp.zeros((n_class, width), F32)
    for k in range(n_class):
        score = jnp.dot(
            rq32 * ck[k : k + 1], same, precision=lax.Precision.HIGHEST, preferred_element_type=F32
        )
        weight = jnp.exp2(score * row_scale)
        numer = numer + weight * cv[k : k + 1]
        denom = denom + weight
    cls_sums[0] = numer
    cls_sums[1] = denom


def notes_tile(flags, labels, width):
    n_rows = flags.shape[1]
    half = n_rows // 2
    same = lax.broadcasted_iota(jnp.int32, (n_rows, n_rows), 0) == lax.broadcasted_iota(
        jnp.int32, (n_rows, n_rows), 1
    )

    def column(row):
        return jnp.sum(jnp.where(same, row, 0.0), axis=1, keepdims=True)

    flag = column(jnp.where(flags == 1, 1.0, 0.0))
    label = column(labels.astype(F32))
    quarter = lax.broadcasted_iota(jnp.int32, (half, width), 1) // (width // 4)
    tile = jnp.where(quarter == 0, flag[:half], label[:half])
    tile = jnp.where(quarter == 2, flag[half:], tile)
    return jnp.where(quarter == 3, label[half:], tile).astype(BF16)


def pack_kernel(axis, feats, n_own, start, with_tile, cells, *refs):
    keep, send = refs[-2:]
    width = cells.shape[2]
    n_dev = keep.shape[0] * 2
    me = lax.axis_index(axis)
    head = 0
    if with_tile:
        tile = notes_tile(refs[0][0:1], refs[0][1:2], width)
        head = tile.shape[0]
    for k in [k for k in range(n_dev) if k % 2] + [k for k in range(n_dev) if k % 2 == 0]:
        at = pl.multiple_of((me ^ k) * n_own, n_own)
        block = cells[:, pl.ds(at, n_own), :][:, start : start + feats]
        out = (keep, send)[k % 2]
        if with_tile:
            out[k // 2, :head] = tile
        out[k // 2, head:] = pltpu.einshape("rfw->frw", block).reshape(-1, width)


def sum_kernel(*refs):
    parts, out = refs[:-1], refs[-1]
    total = parts[0][...].astype(F32)
    for p in parts[1:]:
        total = total + p[...].astype(F32)
    out[...] = total.astype(out.dtype)


def sort_refs(refs, order):
    return [refs[order.index(i)] for i in range(len(order))], refs[len(order) :]


def in_groups(count, step, body):
    step = count if count <= step else math.gcd(count, step)
    if step == count:
        for i in range(count):
            body(i)
        return

    def turn(t, carry):
        for i in range(step):
            body(t * step + i)
        return carry

    lax.fori_loop(0, count // step, turn, 0)


def column_kernel(order, n_feat, n_rows, head, first, last, *refs):
    sources, refs = sort_refs(refs, order)
    if not first:
        before, refs = refs[0], refs[1:]
    col_q, fold, fold_base, row_qv, mask_ref, out, xt_store, y_store, g_store, p_store, w_store, v_store = refs
    width = mask_ref.shape[1]
    n_total = mask_ref.shape[0]
    n_induce = fold_base.shape[0]
    n_weights = row_qv.shape[0] - width
    n_class = n_weights // ROW_HEADS
    full = n_class * width
    head_width = width // ROW_HEADS

    def induce(f):
        cut = pl.ds(pl.multiple_of(head + f * n_rows, n_rows // 2), n_rows)
        x = jnp.concatenate(
            [
                s[:, part, cut, :].reshape(-1, width)
                for part in range(sources[0].shape[1])
                for s in sources
            ],
            axis=0,
        )
        xt = x.T
        xt_store[f] = xt
        mask = mask_ref[...]
        p = jnp.exp2(dot(col_q[...], xt)).astype(BF16)
        sums = dot(p, jnp.concatenate([x * mask, mask], axis=1))
        y = (sums[:, :width] / sums[:, width:]).astype(BF16)
        rows = pl.ds(pl.multiple_of(f * n_induce, n_induce), n_induce)
        for h in range(HEADS):
            y_store[rows, h * width : (h + 1) * width] = y[h * n_induce : (h + 1) * n_induce]

    in_groups(n_feat, 12, induce)

    for j in range(HEADS):
        lanes = slice(2 * j * width, (2 * j + 2) * width)
        both = dot(y_store[...], fold[:, lanes])
        for f in range(n_feat):
            part = (both[f * n_induce : (f + 1) * n_induce] + fold_base[:, lanes]).astype(BF16)
            for i in range(2):
                h = 2 * j + i
                g_store[f, h * n_induce : (h + 1) * n_induce] = part[:, i * width : (i + 1) * width]

    part_lanes = math.gcd(n_total, 512)
    pieces = [
        (f, slice(at, at + part_lanes))
        for f in range(n_feat)
        for at in range(0, n_total, part_lanes)
    ]

    def weigh(i):
        f, lanes = pieces[i]
        x = xt_store[f, :, lanes]
        for h in range(0, HEADS, HEAD_STEP):
            s = jnp.exp2(dot(g_store[f, h * n_induce : (h + HEAD_STEP) * n_induce], x))
            for j in range(HEAD_STEP):
                part = s[j * n_induce : (j + 1) * n_induce]
                part = part * (1.0 / jnp.sum(part, axis=0, keepdims=True))
                p_store[i % P_SLOTS, (h + j) * n_induce : (h + j + 1) * n_induce] = part.astype(BF16)

    def attend(i, o):
        f, lanes = pieces[i]
        res = xt_store[f, :, lanes].astype(F32) + dot(o, p_store[i % P_SLOTS])
        mean = jnp.sum(res * res, axis=0, keepdims=True) * (1.0 / width)
        e = (res * lax.rsqrt(mean + EPSILON)).astype(BF16)
        wv = dot(row_qv[...], e)
        w_store[f, :, lanes] = jnp.exp2(wv[:n_weights])
        v_store[f, :, lanes] = wv[n_weights:]

    weigh(0)
    weigh(1)
    for i in range(len(pieces)):
        if i + 2 < len(pieces):
            weigh(i + 2)
        if i % (n_total // part_lanes) == 0:
            o = g_store[pieces[i][0], HEADS * n_induce :].T
        attend(i, o)

    step = min(n_total, 512)
    for at in range(0, n_total, step):
        lanes = slice(at, at + step)
        denom = w_store[0, :, lanes]
        for f in range(1, n_feat):
            denom = denom + w_store[f, :, lanes]
        if not first:
            denom = denom + before[full:, lanes]
        blocks = [[None] * ROW_HEADS for _ in range(n_class)]
        for h in range(ROW_HEADS):
            begin = [c * width + h * head_width for c in range(n_class)]
            acc = [None if first else before[b : b + head_width, lanes] for b in begin]
            for f in range(n_feat):
                v = v_store[f, h * head_width : (h + 1) * head_width, lanes]
                for c in range(n_class):
                    term = w_store[f, pl.ds(c * ROW_HEADS + h, 1), lanes] * v
                    acc[c] = term if acc[c] is None else acc[c] + term
            for c in range(n_class):
                if last:
                    blocks[c][h] = acc[c].astype(BF16)
                else:
                    out[begin[c] : begin[c] + head_width, lanes] = acc[c]
        if not last:
            out[full:, lanes] = denom
            continue
        for c in range(n_class):
            out[lanes, c * width : (c + 1) * width] = jnp.concatenate(blocks[c], axis=0).T
        padded = jnp.concatenate([denom, jnp.zeros((width - n_weights, step), F32)], axis=0)
        out[lanes, full:] = padded.astype(BF16).T


def notes_kernel(order, head, *refs):
    sources, (mask_out, mask_row, label_row) = sort_refs(refs, order)
    width = mask_out.shape[1]
    tile = jnp.concatenate(
        [s[:, part, :head, :] for part in range(sources[0].shape[1]) for s in sources], axis=0
    ).astype(F32)

    def spread(quarter):
        pieces = [
            jnp.broadcast_to(tile[:, :, q * (width // 4) : q * (width // 4) + 1], tile.shape)
            for q in (quarter, quarter + 2)
        ]
        return jnp.concatenate(pieces, axis=1).reshape(mask_out.shape)

    mask = spread(0)
    mask_out[...] = (mask * 0.125).astype(BF16)
    mask_row[...] = mask.T[: mask_row.shape[0]]
    label_row[...] = spread(1).T[: label_row.shape[0]]


def row_kernel(
    paired, own, other, flags, labels, cls_sums, class_tokens, row_out, table, embed, icl_in
):
    n_class, width = class_tokens.shape
    full = n_class * width
    if paired:
        total = jnp.concatenate(
            [own[p].astype(F32) + other[1 - p].astype(F32) for p in range(2)], axis=0
        )
    else:
        total = jnp.sum(own[...].astype(F32), axis=0)
    lane = lax.broadcasted_iota(jnp.int32, (width, full), 1) // (width // ROW_HEADS)
    spread = (lax.broadcasted_iota(jnp.int32, (width, full), 0) == lane).astype(F32)
    denom = jnp.dot(
        total[:, full:], spread, precision=lax.Precision.HIGHEST, preferred_element_type=F32
    )
    pieces = []
    for c in range(n_class):
        lanes = slice(c * width, (c + 1) * width)
        mix = (total[:, lanes] + cls_sums[0, c : c + 1]) / (
            denom[:, lanes] + cls_sums[1, c : c + 1]
        )
        pieces.append(
            class_tokens[c : c + 1].astype(F32) + dot(mix.astype(BF16), row_out[2])
        )
    row_embed = jnp.concatenate(pieces, axis=1).astype(BF16)
    embed[...] = row_embed[: embed.shape[0]]
    classes, n_rows = table.shape[0], icl_in.shape[0]
    number = lax.broadcasted_iota(jnp.int32, (classes, n_rows), 0).astype(F32)
    hot = number == labels[0:1, :n_rows].astype(F32)
    hot = jnp.where(hot & (flags[0:1, :n_rows].astype(F32) == 1.0), 1.0, 0.0).astype(F32)
    label = lax.dot_general(hot, table[...].astype(F32), TN, preferred_element_type=F32)
    icl_in[...] = (row_embed.astype(F32) + label).astype(BF16)


def query_kernel(embed, icl_query, icl_kvo, turned_query):
    n_rows, full = embed.shape
    query = dot(embed[...], icl_query[...]).astype(BF16)
    head = full // HEADS
    scale = LOG2E / math.sqrt(head)
    for h in range(HEADS):
        lanes = slice(h * head, (h + 1) * head)
        turned_query[h * n_rows : (h + 1) * n_rows] = (
            dot_nt(query[:, lanes], icl_kvo[0, :, lanes]) * scale
        ).astype(BF16)


def icl_kernel(order, *refs):
    parts, (turned_query, mask_row, embed, icl_kvo, out) = sort_refs(refs, order)
    rows = jnp.concatenate([r[...] for r in parts], axis=0)
    full = rows.shape[1]
    n_rows = embed.shape[0]
    head = full // HEADS
    s = dot_nt(turned_query[...], rows)
    s = jnp.where(mask_row[0:1] > 0.5, s, -1e30)
    p = jnp.exp2(s - jnp.max(s, axis=1, keepdims=True))
    denom = jnp.sum(p, axis=1, keepdims=True)
    y = (dot(p.astype(BF16), rows) / denom).astype(BF16)
    mix = jnp.concatenate(
        [
            dot(y[h * n_rows : (h + 1) * n_rows], icl_kvo[1, :, h * head : (h + 1) * head])
            for h in range(HEADS)
        ],
        axis=1,
    ).astype(BF16)
    out[...] = (embed[...].astype(F32) + dot(mix, icl_kvo[2])).astype(BF16)


def call(kernel, outs, *args, scratch=(), mib=16, cost=None, name=None):
    return pl.pallas_call(
        kernel,
        out_shape=tuple(jax.ShapeDtypeStruct(s, d) for s, d in outs),
        in_specs=[pl.BlockSpec(memory_space=pltpu.VMEM)] * len(args),
        out_specs=tuple(pl.BlockSpec(memory_space=pltpu.VMEM) for _ in outs),
        scratch_shapes=scratch,
        compiler_params=pltpu.CompilerParams(vmem_limit_bytes=mib * 1024 * 1024),
        cost_estimate=cost,
        name=name,
    )(*args)


def swap(x, distance):
    n_dev = lax.axis_size("row")
    return lax.ppermute(x, "row", [(s, s ^ distance) for s in range(n_dev)])


CHUNKS = (8, 8)
HEAD_STEP = 2
P_SLOTS = 8
ORDER = (2, 6, 4, 3, 5, 7, 1)
Z_ORDER = (2, 3, 1)


def on_device(
    cells,
    is_context,
    labels,
    inducing,
    induce_query,
    column_kvo,
    cell_qkvo,
    class_tokens,
    class_query,
    row_kvo,
    label_table,
    icl_query,
    icl_kvo,
):
    n_rows, n_feat, width = cells.shape
    n_induce = inducing.shape[0]
    n_class = class_tokens.shape[0]
    n_dev = lax.axis_size("row")
    n_split = lax.axis_size("feat")
    own_feat = n_feat // n_dev
    n_total = n_dev * n_rows
    local_rows = n_rows // n_split
    full = n_class * width
    n_weights = n_class * ROW_HEADS
    paired = n_split == 1 and n_dev == 16

    prepared = call(
        prep_kernel,
        [
            ((HEADS * n_induce, width), BF16),
            ((HEADS * width, 2 * HEADS * width), BF16),
            ((n_induce, 2 * HEADS * width), F32),
            ((n_weights + width, width), BF16),
            ((2, n_class, width), F32),
        ],
        inducing, induce_query, column_kvo, cell_qkvo, class_tokens, class_query, row_kvo,
        name="prep",
    )
    folded, cls_sums = prepared[:4], prepared[4]

    head = n_rows // 2
    chunks = CHUNKS if paired and sum(CHUNKS) == own_feat else (own_feat,)
    chips = n_dev // 2
    groups = []
    if paired:
        order = (0,) + ORDER
        at = 0
        notes = jnp.stack([is_context, labels])
        for c, n in enumerate(chunks):
            top = 0 if c else head
            keep, send = call(
                functools.partial(pack_kernel, "row", n, own_feat, at, c == 0),
                [((chips, top + n * n_rows, width), BF16)] * 2,
                cells, *(() if c else (notes,)),
                mib=8, name="pack",
            )
            got = swap(send, 1)
            both = jnp.stack([keep, got], axis=1)
            groups.append([both[:1]] + [swap(both[q : q + 1], 2 * q) for q in ORDER])
            at += n
    else:
        order = (0,)
        by_feat = jnp.transpose(cells, (1, 0, 2)).reshape(n_dev, own_feat * n_rows, width)
        flags = jnp.where(is_context == 1, 1.0, 0.0).astype(BF16).reshape(2, head)
        tile = jnp.repeat(flags.T, width // 2, axis=1)
        payload = jnp.concatenate(
            [jnp.broadcast_to(tile[None], (n_dev,) + tile.shape), by_feat], axis=1
        )
        got = lax.all_to_all(payload, "row", split_axis=0, concat_axis=0, tiled=True)
        groups.append([got[:, None]])

    mask, mask_row, label_row = call(
        functools.partial(notes_kernel, order, head),
        [((n_total, width), BF16), ((8, n_total), F32), ((8, n_total), F32)],
        *groups[0],
        name="notes",
    )
    state = ()
    for c, n in enumerate(chunks):
        last = c == len(chunks) - 1
        state = call(
            functools.partial(column_kernel, order, n, n_rows, 0 if c else head, c == 0, last),
            [((n_total, full + width), BF16) if last else ((full + n_weights, n_total), F32)],
            *groups[c], *state, *folded, mask,
            scratch=[
                pltpu.VMEM((n, width, n_total), BF16),
                pltpu.VMEM((n * n_induce, HEADS * width), BF16),
                pltpu.VMEM((n, 2 * HEADS * n_induce, width), BF16),
                pltpu.VMEM((P_SLOTS, HEADS * n_induce, math.gcd(n_total, 512)), BF16),
                pltpu.VMEM((n, n_weights, n_total), F32),
                pltpu.VMEM((n, width, n_total), F32),
            ],
            mib=24,
            cost=pl.CostEstimate(
                flops=n * n_total * width * 4000, transcendentals=0, bytes_accessed=4 * 1024 * 1024
            ),
            name="column",
        )
    (partial,) = state

    if paired:
        half = partial.reshape(2, chips, n_rows, full + width)
        (sums,) = call(
            sum_kernel, [(half.shape[1:], BF16)], half[0], swap(half[1], 1), name="sum"
        )
        sums = sums.reshape(chips // 2, 2, n_rows, full + width)
        (own,) = call(
            sum_kernel,
            [(sums.shape[1:], BF16)],
            sums[0], *[swap(sums[z], 4 * z) for z in Z_ORDER],
            name="sum",
        )
        other = swap(own, 2)
        own_flags, own_labels, near = mask_row, label_row, 2 * n_rows
    else:
        own = lax.all_to_all(
            partial.reshape(n_dev * n_split, local_rows, full + width),
            ("row", "feat"), split_axis=0, concat_axis=0, tiled=True,
        )
        other = cls_sums
        own_flags = lax.dynamic_slice_in_dim(
            is_context, lax.axis_index("feat") * local_rows, local_rows
        ).reshape(1, local_rows)
        own_labels, near = labels.reshape(1, local_rows), local_rows
    embed, icl_in = call(
        functools.partial(row_kernel, paired),
        [((local_rows, full), BF16), ((near, full), BF16)],
        own, other, own_flags, own_labels, cls_sums, class_tokens, row_kvo, label_table,
        name="row",
    )
    if paired:
        z_order = (0,) + Z_ORDER
        mine = [icl_in] + [swap(icl_in, 4 * z) for z in Z_ORDER]
        rows = mine + [swap(r, 1) for r in mine]
        row_order = z_order + tuple(chips // 2 + z for z in z_order)
    else:
        rows = (lax.all_gather(icl_in, ("row", "feat"), axis=0, tiled=True),)
        row_order = (0,)
    (turned_query,) = call(
        query_kernel,
        [((HEADS * local_rows, full), BF16)],
        embed, icl_query, icl_kvo,
        name="query",
    )
    (out,) = call(
        functools.partial(icl_kernel, row_order),
        [((local_rows, full), BF16)],
        *rows, turned_query, mask_row, embed, icl_kvo,
        name="icl",
    )
    return out


def solution(mesh):
    return jax.shard_map(
        on_device,
        mesh=mesh,
        in_specs=(
            P(("group", "row"), "feat", None),
            P(("group", "row")),
            P(("group", "row", "feat")),
            P(), P(), P(), P(), P(), P(), P(), P(), P(), P(),
        ),
        out_specs=P(("group", "row", "feat"), None),
        check_vma=False,
    )
```

```python
import functools
import math

import jax
import jax.numpy as jnp
from jax import lax
from jax.experimental import pallas as pl
from jax.experimental.pallas import tpu as pltpu
from jax.sharding import PartitionSpec as P

HEADS = 4
ROW_HEADS = 8
EPSILON = 1e-06
LOG2E = math.log2(math.e)
F32 = jnp.float32
BF16 = jnp.bfloat16
NT = (((1,), (1,)), ((), ()))
TN = (((0,), (0,)), ((), ()))


def dot(a, b):
    return jnp.dot(a, b, preferred_element_type=F32)


def dot_nt(a, b):
    return lax.dot_general(a, b, NT, preferred_element_type=F32)


def head_rows(x, heads):
    width = x.shape[-1]
    lane = lax.broadcasted_iota(jnp.int32, x.shape, 1) // (width // heads)
    x = x.astype(F32)
    return jnp.concatenate(
        [jnp.where(lane == h, x, 0.0) for h in range(heads)], axis=0
    ).astype(BF16)


def prep_kernel(
    inducing,
    induce_query,
    column_kvo,
    cell_qkvo,
    class_tokens,
    class_query,
    row_kvo,
    col_q,
    fold,
    fold_base,
    row_qv,
    cls_sums,
):
    n_induce, width = inducing.shape
    scale = LOG2E / math.sqrt(width // HEADS)
    row_scale = LOG2E / math.sqrt(width // ROW_HEADS)
    iq = dot(inducing[...], induce_query[...]).astype(BF16)
    col_q[...] = (dot_nt(head_rows(iq, HEADS), column_kvo[0]) * scale).astype(BF16)
    mixed = dot(head_rows(column_kvo[1], HEADS), column_kvo[2]).astype(BF16)
    both = jnp.concatenate([mixed, inducing[...]], axis=0)
    keys = dot(both, cell_qkvo[1])
    values = dot(both, cell_qkvo[2])
    n_mixed = mixed.shape[0]
    n_both = n_mixed + n_induce
    g = dot_nt(head_rows(keys, HEADS), cell_qkvo[0]) * scale
    o = dot(head_rows(values, HEADS), cell_qkvo[3])
    for h in range(HEADS):
        for part, at in ((g, 0), (o, HEADS * width)):
            block = part[h * n_both : (h + 1) * n_both]
            lanes = slice(at + h * width, at + (h + 1) * width)
            fold[:, lanes] = block[:n_mixed].astype(BF16)
            fold_base[:, lanes] = block[n_mixed:]
    n_class = class_tokens.shape[0]
    tokens = class_tokens[...]
    rq = dot(tokens, class_query[...]).astype(BF16)
    lane = lax.broadcasted_iota(jnp.int32, (ROW_HEADS, width), 1) // (width // ROW_HEADS)
    head = lax.broadcasted_iota(jnp.int32, (ROW_HEADS, width), 0)
    rq32 = rq.astype(F32)
    blocks = jnp.concatenate(
        [jnp.where(lane == head, rq32[c : c + 1], 0.0) for c in range(n_class)], axis=0
    ).astype(BF16)
    row_qv[: n_class * ROW_HEADS] = (dot_nt(blocks, row_kvo[0]) * row_scale).astype(BF16)
    row_qv[n_class * ROW_HEADS :] = row_kvo[1].astype(F32).T.astype(BF16)
    ck = dot(tokens, row_kvo[0]).astype(BF16).astype(F32)
    cv = dot(tokens, row_kvo[1]).astype(BF16).astype(F32)
    same = (
        lax.broadcasted_iota(jnp.int32, (width, width), 0) // (width // ROW_HEADS)
        == lax.broadcasted_iota(jnp.int32, (width, width), 1) // (width // ROW_HEADS)
    ).astype(F32)
    numer = jnp.zeros((n_class, width), F32)
    denom = jnp.zeros((n_class, width), F32)
    for k in range(n_class):
        score = jnp.dot(
            rq32 * ck[k : k + 1], same, precision=lax.Precision.HIGHEST, preferred_element_type=F32
        )
        weight = jnp.exp2(score * row_scale)
        numer = numer + weight * cv[k : k + 1]
        denom = denom + weight
    cls_sums[0] = numer
    cls_sums[1] = denom


def notes_tile(flags, labels, width):
    n_rows = flags.shape[1]
    half = n_rows // 2
    same = lax.broadcasted_iota(jnp.int32, (n_rows, n_rows), 0) == lax.broadcasted_iota(
        jnp.int32, (n_rows, n_rows), 1
    )

    def column(row):
        return jnp.sum(jnp.where(same, row, 0.0), axis=1, keepdims=True)

    flag = column(jnp.where(flags == 1, 1.0, 0.0))
    label = column(labels.astype(F32))
    quarter = lax.broadcasted_iota(jnp.int32, (half, width), 1) // (width // 4)
    tile = jnp.where(quarter == 0, flag[:half], label[:half])
    tile = jnp.where(quarter == 2, flag[half:], tile)
    return jnp.where(quarter == 3, label[half:], tile).astype(BF16)


def pack_kernel(axis, feats, n_own, start, with_tile, cells, *refs):
    keep, send = refs[-2:]
    width = cells.shape[2]
    n_dev = keep.shape[0] * 2
    me = lax.axis_index(axis)
    head = 0
    if with_tile:
        tile = notes_tile(refs[0][0:1], refs[0][1:2], width)
        head = tile.shape[0]
    for k in [k for k in range(n_dev) if k % 2] + [k for k in range(n_dev) if k % 2 == 0]:
        at = pl.multiple_of((me ^ k) * n_own, n_own)
        block = cells[:, pl.ds(at, n_own), :][:, start : start + feats]
        out = (keep, send)[k % 2]
        if with_tile:
            out[k // 2, :head] = tile
        out[k // 2, head:] = pltpu.einshape("rfw->frw", block).reshape(-1, width)


def sum_kernel(*refs):
    parts, out = refs[:-1], refs[-1]
    total = parts[0][...].astype(F32)
    for p in parts[1:]:
        total = total + p[...].astype(F32)
    out[...] = total.astype(out.dtype)


def sort_refs(refs, order):
    return [refs[order.index(i)] for i in range(len(order))], refs[len(order) :]


def in_groups(count, step, body):
    step = count if count <= step else math.gcd(count, step)
    if step == count:
        for i in range(count):
            body(i)
        return

    def turn(t, carry):
        for i in range(step):
            body(t * step + i)
        return carry

    lax.fori_loop(0, count // step, turn, 0)


def column_kernel(order, n_feat, n_rows, head, first, last, compact, *refs):
    sources, refs = sort_refs(refs, order)
    if not first:
        before, refs = refs[0], refs[1:]
    col_q, fold, fold_base, row_qv, mask_ref, out, xt_store, y_store, g_store, p_store, w_store, v_store = refs
    width = mask_ref.shape[1]
    n_total = mask_ref.shape[0]
    n_induce = fold_base.shape[0]
    n_weights = row_qv.shape[0] - width
    n_class = n_weights // ROW_HEADS
    full = n_class * width
    head_width = width // ROW_HEADS

    def induce(f):
        cut = pl.ds(pl.multiple_of(head + f * n_rows, n_rows // 2), n_rows)
        x = jnp.concatenate(
            [
                s[:, part, cut, :].reshape(-1, width)
                for part in range(sources[0].shape[1])
                for s in sources
            ],
            axis=0,
        )
        xt = x.T
        xt_store[f] = xt
        mask = mask_ref[...]
        p = jnp.exp2(dot(col_q[...], xt)).astype(BF16)
        sums = dot(p, jnp.concatenate([x * mask, mask], axis=1))
        y = (sums[:, :width] / sums[:, width:]).astype(BF16)
        rows = pl.ds(pl.multiple_of(f * n_induce, n_induce), n_induce)
        for h in range(HEADS):
            y_store[rows, h * width : (h + 1) * width] = y[h * n_induce : (h + 1) * n_induce]

    in_groups(n_feat, 12, induce)

    for j in range(HEADS):
        lanes = slice(2 * j * width, (2 * j + 2) * width)
        both = dot(y_store[...], fold[:, lanes])
        for f in range(n_feat):
            part = (both[f * n_induce : (f + 1) * n_induce] + fold_base[:, lanes]).astype(BF16)
            for i in range(2):
                h = 2 * j + i
                g_store[f, h * n_induce : (h + 1) * n_induce] = part[:, i * width : (i + 1) * width]

    part_lanes = math.gcd(n_total, 512)
    pieces = [
        (f, slice(at, at + part_lanes))
        for f in range(n_feat)
        for at in range(0, n_total, part_lanes)
    ]

    def weigh(i):
        f, lanes = pieces[i]
        x = xt_store[f, :, lanes]
        for h in range(0, HEADS, HEAD_STEP):
            s = jnp.exp2(dot(g_store[f, h * n_induce : (h + HEAD_STEP) * n_induce], x))
            for j in range(HEAD_STEP):
                part = s[j * n_induce : (j + 1) * n_induce]
                part = part * (1.0 / jnp.sum(part, axis=0, keepdims=True))
                p_store[i % P_SLOTS, (h + j) * n_induce : (h + j + 1) * n_induce] = part.astype(BF16)

    def attend(i, o):
        f, lanes = pieces[i]
        res = xt_store[f, :, lanes].astype(F32) + dot(o, p_store[i % P_SLOTS])
        mean = jnp.sum(res * res, axis=0, keepdims=True) * (1.0 / width)
        e = (res * lax.rsqrt(mean + EPSILON)).astype(BF16)
        wv = dot(row_qv[...], e)
        w_store[f, :, lanes] = jnp.exp2(wv[:n_weights])
        v_store[f, :, lanes] = wv[n_weights:]

    weigh(0)
    weigh(1)
    for i in range(len(pieces)):
        if i + 2 < len(pieces):
            weigh(i + 2)
        if i % (n_total // part_lanes) == 0:
            o = g_store[pieces[i][0], HEADS * n_induce :].T
        attend(i, o)

    step = min(n_total, 512)
    for at in range(0, n_total, step):
        lanes = slice(at, at + step)
        denom = w_store[0, :, lanes]
        for f in range(1, n_feat):
            denom = denom + w_store[f, :, lanes]
        if not first:
            denom = denom + before[full:, lanes]
        blocks = [[None] * ROW_HEADS for _ in range(n_class)]
        for h in range(ROW_HEADS):
            begin = [c * width + h * head_width for c in range(n_class)]
            acc = [None if first else before[b : b + head_width, lanes] for b in begin]
            for f in range(n_feat):
                v = v_store[f, h * head_width : (h + 1) * head_width, lanes]
                for c in range(n_class):
                    term = w_store[f, pl.ds(c * ROW_HEADS + h, 1), lanes] * v
                    acc[c] = term if acc[c] is None else acc[c] + term
            for c in range(n_class):
                if last:
                    blocks[c][h] = acc[c].astype(BF16)
                else:
                    out[begin[c] : begin[c] + head_width, lanes] = acc[c]
        if not last:
            out[full:, lanes] = denom
            continue
        if compact:
            block = width // n_class
            for c in range(n_class):
                turned = jnp.concatenate(blocks[c], axis=0).T
                for k in range(step // block):
                    out[at // block + k, c * block : (c + 1) * block] = (
                        turned[k * block : (k + 1) * block]
                    )
            group = lax.broadcasted_iota(jnp.int32, (ROW_HEADS, width), 1) // block
            for k in range(step // block):
                tile = slice(k // n_class * width, (k // n_class + 1) * width)
                line = jnp.zeros((ROW_HEADS, width), F32)
                for c in range(n_class):
                    part = denom[c * ROW_HEADS : (c + 1) * ROW_HEADS, tile]
                    shift = (c - k) % n_class * block
                    part = pltpu.roll(part, shift, 1) if shift else part
                    line = jnp.where(group == c, part, line)
                out[at // block + k, width:] = line.astype(BF16)
            continue
        for c in range(n_class):
            out[lanes, c * width : (c + 1) * width] = jnp.concatenate(blocks[c], axis=0).T
        padded = jnp.concatenate([denom, jnp.zeros((width - n_weights, step), F32)], axis=0)
        out[lanes, full:] = padded.astype(BF16).T


def notes_kernel(order, head, *refs):
    sources, (mask_out, mask_row, label_row) = sort_refs(refs, order)
    width = mask_out.shape[1]
    tile = jnp.concatenate(
        [s[:, part, :head, :] for part in range(sources[0].shape[1]) for s in sources], axis=0
    ).astype(F32)

    def spread(quarter):
        pieces = [
            jnp.broadcast_to(tile[:, :, q * (width // 4) : q * (width // 4) + 1], tile.shape)
            for q in (quarter, quarter + 2)
        ]
        return jnp.concatenate(pieces, axis=1).reshape(mask_out.shape)

    mask = spread(0)
    mask_out[...] = (mask * 0.125).astype(BF16)
    mask_row[...] = mask.T[: mask_row.shape[0]]
    label_row[...] = spread(1).T[: label_row.shape[0]]


def row_kernel(
    paired, own, other, flags, labels, cls_sums, class_tokens, row_out, table, embed, icl_in
):
    n_class, width = class_tokens.shape
    full = n_class * width
    pieces = []
    if paired:
        block = width // n_class
        totals = [own[p].astype(F32) + other[1 - p].astype(F32) for p in range(2)]
        lane = lax.broadcasted_iota(jnp.int32, (ROW_HEADS, width), 1) // (width // ROW_HEADS)
        spread = (lax.broadcasted_iota(jnp.int32, (ROW_HEADS, width), 0) == lane).astype(F32)
        denoms = [
            lax.dot_general(
                t[width:], spread, TN,
                precision=lax.Precision.HIGHEST, preferred_element_type=F32,
            )
            for t in totals
        ]
        for c in range(n_class):
            rows = slice(c * block, (c + 1) * block)
            pieces.append(
                (
                    jnp.concatenate([t[rows] for t in totals], axis=0),
                    jnp.concatenate([d[rows] for d in denoms], axis=0),
                )
            )
    else:
        total = jnp.sum(own[...].astype(F32), axis=0)
        lane = lax.broadcasted_iota(jnp.int32, (width, full), 1) // (width // ROW_HEADS)
        spread = (lax.broadcasted_iota(jnp.int32, (width, full), 0) == lane).astype(F32)
        denom = jnp.dot(
            total[:, full:], spread, precision=lax.Precision.HIGHEST, preferred_element_type=F32
        )
        for c in range(n_class):
            lanes = slice(c * width, (c + 1) * width)
            pieces.append((total[:, lanes], denom[:, lanes]))
    for c, (numer, denom) in enumerate(pieces):
        mix = (numer + cls_sums[0, c : c + 1]) / (denom + cls_sums[1, c : c + 1])
        pieces[c] = class_tokens[c : c + 1].astype(F32) + dot(mix.astype(BF16), row_out[2])
    row_embed = jnp.concatenate(pieces, axis=1).astype(BF16)
    embed[...] = row_embed[: embed.shape[0]]
    classes, n_rows = table.shape[0], icl_in.shape[0]
    number = lax.broadcasted_iota(jnp.int32, (classes, n_rows), 0).astype(F32)
    hot = number == labels[0:1, :n_rows].astype(F32)
    hot = jnp.where(hot & (flags[0:1, :n_rows].astype(F32) == 1.0), 1.0, 0.0).astype(F32)
    label = lax.dot_general(hot, table[...].astype(F32), TN, preferred_element_type=F32)
    icl_in[...] = (row_embed.astype(F32) + label).astype(BF16)


def query_kernel(embed, icl_query, icl_kvo, turned_query):
    n_rows, full = embed.shape
    query = dot(embed[...], icl_query[...]).astype(BF16)
    head = full // HEADS
    scale = LOG2E / math.sqrt(head)
    for h in range(HEADS):
        lanes = slice(h * head, (h + 1) * head)
        turned_query[h * n_rows : (h + 1) * n_rows] = (
            dot_nt(query[:, lanes], icl_kvo[0, :, lanes]) * scale
        ).astype(BF16)


def icl_kernel(order, *refs):
    parts, (turned_query, mask_row, embed, icl_kvo, out) = sort_refs(refs, order)
    rows = jnp.concatenate([r[...] for r in parts], axis=0)
    full = rows.shape[1]
    n_rows = embed.shape[0]
    head = full // HEADS
    s = dot_nt(turned_query[...], rows)
    s = jnp.where(mask_row[0:1] > 0.5, s, -1e30)
    p = jnp.exp2(s - jnp.max(s, axis=1, keepdims=True))
    denom = jnp.sum(p, axis=1, keepdims=True)
    y = (dot(p.astype(BF16), rows) / denom).astype(BF16)
    mix = jnp.concatenate(
        [
            dot(y[h * n_rows : (h + 1) * n_rows], icl_kvo[1, :, h * head : (h + 1) * head])
            for h in range(HEADS)
        ],
        axis=1,
    ).astype(BF16)
    out[...] = (embed[...].astype(F32) + dot(mix, icl_kvo[2])).astype(BF16)


def call(kernel, outs, *args, scratch=(), mib=16, cost=None, name=None):
    return pl.pallas_call(
        kernel,
        out_shape=tuple(jax.ShapeDtypeStruct(s, d) for s, d in outs),
        in_specs=[pl.BlockSpec(memory_space=pltpu.VMEM)] * len(args),
        out_specs=tuple(pl.BlockSpec(memory_space=pltpu.VMEM) for _ in outs),
        scratch_shapes=scratch,
        compiler_params=pltpu.CompilerParams(vmem_limit_bytes=mib * 1024 * 1024),
        cost_estimate=cost,
        name=name,
    )(*args)


def swap(x, distance):
    n_dev = lax.axis_size("row")
    return lax.ppermute(x, "row", [(s, s ^ distance) for s in range(n_dev)])


CHUNKS = (8, 8)
HEAD_STEP = 2
P_SLOTS = 8
ORDER = (2, 6, 4, 3, 5, 7, 1)
Z_ORDER = (2, 3, 1)


def on_device(
    cells,
    is_context,
    labels,
    inducing,
    induce_query,
    column_kvo,
    cell_qkvo,
    class_tokens,
    class_query,
    row_kvo,
    label_table,
    icl_query,
    icl_kvo,
):
    n_rows, n_feat, width = cells.shape
    n_induce = inducing.shape[0]
    n_class = class_tokens.shape[0]
    n_dev = lax.axis_size("row")
    n_split = lax.axis_size("feat")
    own_feat = n_feat // n_dev
    n_total = n_dev * n_rows
    local_rows = n_rows // n_split
    full = n_class * width
    n_weights = n_class * ROW_HEADS
    paired = n_split == 1 and n_dev == 16 and n_rows * n_class == width

    prepared = call(
        prep_kernel,
        [
            ((HEADS * n_induce, width), BF16),
            ((HEADS * width, 2 * HEADS * width), BF16),
            ((n_induce, 2 * HEADS * width), F32),
            ((n_weights + width, width), BF16),
            ((2, n_class, width), F32),
        ],
        inducing, induce_query, column_kvo, cell_qkvo, class_tokens, class_query, row_kvo,
        name="prep",
    )
    folded, cls_sums = prepared[:4], prepared[4]

    head = n_rows // 2
    chunks = CHUNKS if paired and sum(CHUNKS) == own_feat else (own_feat,)
    chips = n_dev // 2
    groups = []
    if paired:
        order = (0,) + ORDER
        at = 0
        notes = jnp.stack([is_context, labels])
        for c, n in enumerate(chunks):
            top = 0 if c else head
            keep, send = call(
                functools.partial(pack_kernel, "row", n, own_feat, at, c == 0),
                [((chips, top + n * n_rows, width), BF16)] * 2,
                cells, *(() if c else (notes,)),
                mib=8, name="pack",
            )
            got = swap(send, 1)
            both = jnp.stack([keep, got], axis=1)
            groups.append([both[:1]] + [swap(both[q : q + 1], 2 * q) for q in ORDER])
            at += n
    else:
        order = (0,)
        by_feat = jnp.transpose(cells, (1, 0, 2)).reshape(n_dev, own_feat * n_rows, width)
        flags = jnp.where(is_context == 1, 1.0, 0.0).astype(BF16).reshape(2, head)
        tile = jnp.repeat(flags.T, width // 2, axis=1)
        payload = jnp.concatenate(
            [jnp.broadcast_to(tile[None], (n_dev,) + tile.shape), by_feat], axis=1
        )
        got = lax.all_to_all(payload, "row", split_axis=0, concat_axis=0, tiled=True)
        groups.append([got[:, None]])

    mask, mask_row, label_row = call(
        functools.partial(notes_kernel, order, head),
        [((n_total, width), BF16), ((8, n_total), F32), ((8, n_total), F32)],
        *groups[0],
        name="notes",
    )
    state = ()
    lines = width + ROW_HEADS
    sent = (n_dev, lines, width) if paired else (n_total, full + width)
    for c, n in enumerate(chunks):
        last = c == len(chunks) - 1
        state = call(
            functools.partial(
                column_kernel, order, n, n_rows, 0 if c else head, c == 0, last, paired
            ),
            [(sent, BF16) if last else ((full + n_weights, n_total), F32)],
            *groups[c], *state, *folded, mask,
            scratch=[
                pltpu.VMEM((n, width, n_total), BF16),
                pltpu.VMEM((n * n_induce, HEADS * width), BF16),
                pltpu.VMEM((n, 2 * HEADS * n_induce, width), BF16),
                pltpu.VMEM((P_SLOTS, HEADS * n_induce, math.gcd(n_total, 512)), BF16),
                pltpu.VMEM((n, n_weights, n_total), F32),
                pltpu.VMEM((n, width, n_total), F32),
            ],
            mib=24,
            cost=pl.CostEstimate(
                flops=n * n_total * width * 4000, transcendentals=0, bytes_accessed=4 * 1024 * 1024
            ),
            name="column",
        )
    (partial,) = state

    if paired:
        half = partial.reshape(2, chips, lines, width)
        (sums,) = call(
            sum_kernel, [(half.shape[1:], BF16)], half[0], swap(half[1], 1), name="sum"
        )
        sums = sums.reshape(chips // 2, 2, lines, width)
        (own,) = call(
            sum_kernel,
            [(sums.shape[1:], BF16)],
            sums[0], *[swap(sums[z], 4 * z) for z in Z_ORDER],
            name="sum",
        )
        other = swap(own, 2)
        own_flags, own_labels, near = mask_row, label_row, 2 * n_rows
    else:
        own = lax.all_to_all(
            partial.reshape(n_dev * n_split, local_rows, full + width),
            ("row", "feat"), split_axis=0, concat_axis=0, tiled=True,
        )
        other = cls_sums
        own_flags = lax.dynamic_slice_in_dim(
            is_context, lax.axis_index("feat") * local_rows, local_rows
        ).reshape(1, local_rows)
        own_labels, near = labels.reshape(1, local_rows), local_rows
    embed, icl_in = call(
        functools.partial(row_kernel, paired),
        [((local_rows, full), BF16), ((near, full), BF16)],
        own, other, own_flags, own_labels, cls_sums, class_tokens, row_kvo, label_table,
        name="row",
    )
    if paired:
        z_order = (0,) + Z_ORDER
        mine = [icl_in] + [swap(icl_in, 4 * z) for z in Z_ORDER]
        rows = mine + [swap(r, 1) for r in mine]
        row_order = z_order + tuple(chips // 2 + z for z in z_order)
    else:
        rows = (lax.all_gather(icl_in, ("row", "feat"), axis=0, tiled=True),)
        row_order = (0,)
    (turned_query,) = call(
        query_kernel,
        [((HEADS * local_rows, full), BF16)],
        embed, icl_query, icl_kvo,
        name="query",
    )
    (out,) = call(
        functools.partial(icl_kernel, row_order),
        [((local_rows, full), BF16)],
        *rows, turned_query, mask_row, embed, icl_kvo,
        name="icl",
    )
    return out


def solution(mesh):
    return jax.shard_map(
        on_device,
        mesh=mesh,
        in_specs=(
            P(("group", "row"), "feat", None),
            P(("group", "row")),
            P(("group", "row", "feat")),
            P(), P(), P(), P(), P(), P(), P(), P(), P(), P(),
        ),
        out_specs=P(("group", "row", "feat"), None),
        check_vma=False,
    )
```

```python
import functools
import math

import jax
import jax.numpy as jnp
from jax import lax
from jax.experimental import pallas as pl
from jax.experimental.pallas import tpu as pltpu
from jax.sharding import PartitionSpec as P

HEADS = 4
ROW_HEADS = 8
EPSILON = 1e-06
LOG2E = math.log2(math.e)
F32 = jnp.float32
BF16 = jnp.bfloat16
NT = (((1,), (1,)), ((), ()))
TN = (((0,), (0,)), ((), ()))


def dot(a, b):
    return jnp.dot(a, b, preferred_element_type=F32)


def dot_nt(a, b):
    return lax.dot_general(a, b, NT, preferred_element_type=F32)


def head_rows(x, heads):
    width = x.shape[-1]
    lane = lax.broadcasted_iota(jnp.int32, x.shape, 1) // (width // heads)
    x = x.astype(F32)
    return jnp.concatenate(
        [jnp.where(lane == h, x, 0.0) for h in range(heads)], axis=0
    ).astype(BF16)


def prep_kernel(
    inducing,
    induce_query,
    column_kvo,
    cell_qkvo,
    class_tokens,
    class_query,
    row_kvo,
    col_q,
    fold,
    fold_base,
    row_qv,
    cls_sums,
):
    n_induce, width = inducing.shape
    scale = LOG2E / math.sqrt(width // HEADS)
    row_scale = LOG2E / math.sqrt(width // ROW_HEADS)
    iq = dot(inducing[...], induce_query[...]).astype(BF16)
    col_q[...] = (dot_nt(head_rows(iq, HEADS), column_kvo[0]) * scale).astype(BF16)
    mixed = dot(head_rows(column_kvo[1], HEADS), column_kvo[2]).astype(BF16)
    both = jnp.concatenate([mixed, inducing[...]], axis=0)
    keys = dot(both, cell_qkvo[1])
    values = dot(both, cell_qkvo[2])
    n_mixed = mixed.shape[0]
    n_both = n_mixed + n_induce
    g = dot_nt(head_rows(keys, HEADS), cell_qkvo[0]) * scale
    o = dot(head_rows(values, HEADS), cell_qkvo[3])
    for h in range(HEADS):
        for part, at in ((g, 0), (o, HEADS * width)):
            block = part[h * n_both : (h + 1) * n_both]
            lanes = slice(at + h * width, at + (h + 1) * width)
            fold[:, lanes] = block[:n_mixed].astype(BF16)
            fold_base[:, lanes] = block[n_mixed:]
    n_class = class_tokens.shape[0]
    tokens = class_tokens[...]
    rq = dot(tokens, class_query[...]).astype(BF16)
    lane = lax.broadcasted_iota(jnp.int32, (ROW_HEADS, width), 1) // (width // ROW_HEADS)
    head = lax.broadcasted_iota(jnp.int32, (ROW_HEADS, width), 0)
    rq32 = rq.astype(F32)
    blocks = jnp.concatenate(
        [jnp.where(lane == head, rq32[c : c + 1], 0.0) for c in range(n_class)], axis=0
    ).astype(BF16)
    row_qv[: n_class * ROW_HEADS] = (dot_nt(blocks, row_kvo[0]) * row_scale).astype(BF16)
    row_qv[n_class * ROW_HEADS :] = row_kvo[1].astype(F32).T.astype(BF16)
    ck = dot(tokens, row_kvo[0]).astype(BF16).astype(F32)
    cv = dot(tokens, row_kvo[1]).astype(BF16).astype(F32)
    same = (
        lax.broadcasted_iota(jnp.int32, (width, width), 0) // (width // ROW_HEADS)
        == lax.broadcasted_iota(jnp.int32, (width, width), 1) // (width // ROW_HEADS)
    ).astype(F32)
    numer = jnp.zeros((n_class, width), F32)
    denom = jnp.zeros((n_class, width), F32)
    for k in range(n_class):
        score = jnp.dot(
            rq32 * ck[k : k + 1], same, precision=lax.Precision.HIGHEST, preferred_element_type=F32
        )
        weight = jnp.exp2(score * row_scale)
        numer = numer + weight * cv[k : k + 1]
        denom = denom + weight
    cls_sums[0] = numer
    cls_sums[1] = denom


def notes_tile(flags, labels, width):
    n_rows = flags.shape[1]
    half = n_rows // 2
    same = lax.broadcasted_iota(jnp.int32, (n_rows, n_rows), 0) == lax.broadcasted_iota(
        jnp.int32, (n_rows, n_rows), 1
    )

    def column(row):
        return jnp.sum(jnp.where(same, row, 0.0), axis=1, keepdims=True)

    flag = column(jnp.where(flags == 1, 1.0, 0.0))
    label = column(labels.astype(F32))
    quarter = lax.broadcasted_iota(jnp.int32, (half, width), 1) // (width // 4)
    tile = jnp.where(quarter == 0, flag[:half], label[:half])
    tile = jnp.where(quarter == 2, flag[half:], tile)
    return jnp.where(quarter == 3, label[half:], tile).astype(BF16)


def pack_kernel(axis, feats, n_own, start, with_tile, cells, *refs):
    keep, send = refs[-2:]
    width = cells.shape[2]
    n_dev = keep.shape[0] * 2
    me = lax.axis_index(axis)
    head = 0
    if with_tile:
        tile = notes_tile(refs[0][0:1], refs[0][1:2], width)
        head = tile.shape[0]
    for k in [k for k in range(n_dev) if k % 2] + [k for k in range(n_dev) if k % 2 == 0]:
        at = pl.multiple_of((me ^ k) * n_own, n_own)
        block = cells[:, pl.ds(at, n_own), :][:, start : start + feats]
        out = (keep, send)[k % 2]
        if with_tile:
            out[k // 2, :head] = tile
        out[k // 2, head:] = pltpu.einshape("rfw->frw", block).reshape(-1, width)


def sum_kernel(*refs):
    parts, out = refs[:-1], refs[-1]
    total = parts[0][...].astype(F32)
    for p in parts[1:]:
        total = total + p[...].astype(F32)
    out[...] = total.astype(out.dtype)


def sort_refs(refs, order):
    return [refs[order.index(i)] for i in range(len(order))], refs[len(order) :]


def in_groups(count, step, body):
    step = count if count <= step else math.gcd(count, step)
    if step == count:
        for i in range(count):
            body(i)
        return

    def turn(t, carry):
        for i in range(step):
            body(t * step + i)
        return carry

    lax.fori_loop(0, count // step, turn, 0)


def column_kernel(order, n_feat, n_rows, head, first, last, compact, *refs):
    sources, refs = sort_refs(refs, order)
    if not first:
        before, refs = refs[0], refs[1:]
    col_q, fold, fold_base, row_qv, mask_ref, out, xt_store, y_store, g_store, p_store, w_store, v_store = refs
    width = mask_ref.shape[1]
    n_total = mask_ref.shape[0]
    n_induce = fold_base.shape[0]
    n_weights = row_qv.shape[0] - width
    n_class = n_weights // ROW_HEADS
    full = n_class * width
    head_width = width // ROW_HEADS

    def induce(f):
        cut = pl.ds(pl.multiple_of(head + f * n_rows, n_rows // 2), n_rows)
        x = jnp.concatenate(
            [
                s[:, part, cut, :].reshape(-1, width)
                for part in range(sources[0].shape[1])
                for s in sources
            ],
            axis=0,
        )
        xt = x.T
        xt_store[f] = xt
        mask = mask_ref[...]
        p = jnp.exp2(dot(col_q[...], xt)).astype(BF16)
        sums = dot(p, jnp.concatenate([x * mask, mask], axis=1))
        y = (sums[:, :width] / sums[:, width:]).astype(BF16)
        rows = pl.ds(pl.multiple_of(f * n_induce, n_induce), n_induce)
        for h in range(HEADS):
            y_store[rows, h * width : (h + 1) * width] = y[h * n_induce : (h + 1) * n_induce]

    in_groups(n_feat, 12, induce)

    for j in range(HEADS):
        lanes = slice(2 * j * width, (2 * j + 2) * width)
        both = dot(y_store[...], fold[:, lanes])
        for f in range(n_feat):
            part = (both[f * n_induce : (f + 1) * n_induce] + fold_base[:, lanes]).astype(BF16)
            for i in range(2):
                h = 2 * j + i
                g_store[f, h * n_induce : (h + 1) * n_induce] = part[:, i * width : (i + 1) * width]

    part_lanes = math.gcd(n_total, 512)
    pieces = [
        (f, slice(at, at + part_lanes))
        for f in range(n_feat)
        for at in range(0, n_total, part_lanes)
    ]

    def weigh(i):
        f, lanes = pieces[i]
        x = xt_store[f, :, lanes]
        for h in range(0, HEADS, HEAD_STEP):
            s = jnp.exp2(dot(g_store[f, h * n_induce : (h + HEAD_STEP) * n_induce], x))
            for j in range(HEAD_STEP):
                part = s[j * n_induce : (j + 1) * n_induce]
                part = part * (1.0 / jnp.sum(part, axis=0, keepdims=True))
                p_store[i % P_SLOTS, (h + j) * n_induce : (h + j + 1) * n_induce] = part.astype(BF16)

    def attend(i, o):
        f, lanes = pieces[i]
        res = xt_store[f, :, lanes].astype(F32) + dot(o, p_store[i % P_SLOTS])
        mean = jnp.sum(res * res, axis=0, keepdims=True) * (1.0 / width)
        e = (res * lax.rsqrt(mean + EPSILON)).astype(BF16)
        wv = dot(row_qv[...], e)
        w_store[f, :, lanes] = jnp.exp2(wv[:n_weights])
        v_store[f, :, lanes] = wv[n_weights:]

    weigh(0)
    weigh(1)
    weigh(2)
    for i in range(len(pieces)):
        if i + 3 < len(pieces):
            weigh(i + 3)
        if i % (n_total // part_lanes) == 0:
            o = g_store[pieces[i][0], HEADS * n_induce :].T
        attend(i, o)

    step = min(n_total, 512)
    for at in range(0, n_total, step):
        lanes = slice(at, at + step)
        denom = w_store[0, :, lanes]
        for f in range(1, n_feat):
            denom = denom + w_store[f, :, lanes]
        if not first:
            denom = denom + before[full:, lanes]
        blocks = [[None] * ROW_HEADS for _ in range(n_class)]
        for h in range(ROW_HEADS):
            begin = [c * width + h * head_width for c in range(n_class)]
            acc = [None if first else before[b : b + head_width, lanes] for b in begin]
            for f in range(n_feat):
                v = v_store[f, h * head_width : (h + 1) * head_width, lanes]
                for c in range(n_class):
                    term = w_store[f, pl.ds(c * ROW_HEADS + h, 1), lanes] * v
                    acc[c] = term if acc[c] is None else acc[c] + term
            for c in range(n_class):
                if last:
                    blocks[c][h] = acc[c].astype(BF16)
                else:
                    out[begin[c] : begin[c] + head_width, lanes] = acc[c]
        if not last:
            out[full:, lanes] = denom
            continue
        if compact:
            block = width // n_class
            for c in range(n_class):
                turned = jnp.concatenate(blocks[c], axis=0).T
                for k in range(step // block):
                    out[at // block + k, c * block : (c + 1) * block] = (
                        turned[k * block : (k + 1) * block]
                    )
            group = lax.broadcasted_iota(jnp.int32, (ROW_HEADS, width), 1) // block
            for k in range(step // block):
                tile = slice(k // n_class * width, (k // n_class + 1) * width)
                line = jnp.zeros((ROW_HEADS, width), F32)
                for c in range(n_class):
                    part = denom[c * ROW_HEADS : (c + 1) * ROW_HEADS, tile]
                    shift = (c - k) % n_class * block
                    part = pltpu.roll(part, shift, 1) if shift else part
                    line = jnp.where(group == c, part, line)
                out[at // block + k, width:] = line.astype(BF16)
            continue
        for c in range(n_class):
            out[lanes, c * width : (c + 1) * width] = jnp.concatenate(blocks[c], axis=0).T
        padded = jnp.concatenate([denom, jnp.zeros((width - n_weights, step), F32)], axis=0)
        out[lanes, full:] = padded.astype(BF16).T


def notes_kernel(order, head, *refs):
    sources, (mask_out, mask_row, label_row) = sort_refs(refs, order)
    width = mask_out.shape[1]
    tile = jnp.concatenate(
        [s[:, part, :head, :] for part in range(sources[0].shape[1]) for s in sources], axis=0
    ).astype(F32)

    def spread(quarter):
        pieces = [
            jnp.broadcast_to(tile[:, :, q * (width // 4) : q * (width // 4) + 1], tile.shape)
            for q in (quarter, quarter + 2)
        ]
        return jnp.concatenate(pieces, axis=1).reshape(mask_out.shape)

    mask = spread(0)
    mask_out[...] = (mask * 0.125).astype(BF16)
    mask_row[...] = mask.T[: mask_row.shape[0]]
    label_row[...] = spread(1).T[: label_row.shape[0]]


def row_kernel(
    paired, own, other, flags, labels, cls_sums, class_tokens, row_out, table, embed, icl_in
):
    n_class, width = class_tokens.shape
    full = n_class * width
    pieces = []
    if paired:
        block = width // n_class
        totals = [own[p].astype(F32) + other[1 - p].astype(F32) for p in range(2)]
        lane = lax.broadcasted_iota(jnp.int32, (ROW_HEADS, width), 1) // (width // ROW_HEADS)
        spread = (lax.broadcasted_iota(jnp.int32, (ROW_HEADS, width), 0) == lane).astype(F32)
        denoms = [
            lax.dot_general(
                t[width:], spread, TN,
                precision=lax.Precision.HIGHEST, preferred_element_type=F32,
            )
            for t in totals
        ]
        for c in range(n_class):
            rows = slice(c * block, (c + 1) * block)
            pieces.append(
                (
                    jnp.concatenate([t[rows] for t in totals], axis=0),
                    jnp.concatenate([d[rows] for d in denoms], axis=0),
                )
            )
    else:
        total = jnp.sum(own[...].astype(F32), axis=0)
        lane = lax.broadcasted_iota(jnp.int32, (width, full), 1) // (width // ROW_HEADS)
        spread = (lax.broadcasted_iota(jnp.int32, (width, full), 0) == lane).astype(F32)
        denom = jnp.dot(
            total[:, full:], spread, precision=lax.Precision.HIGHEST, preferred_element_type=F32
        )
        for c in range(n_class):
            lanes = slice(c * width, (c + 1) * width)
            pieces.append((total[:, lanes], denom[:, lanes]))
    for c, (numer, denom) in enumerate(pieces):
        mix = (numer + cls_sums[0, c : c + 1]) / (denom + cls_sums[1, c : c + 1])
        pieces[c] = class_tokens[c : c + 1].astype(F32) + dot(mix.astype(BF16), row_out[2])
    row_embed = jnp.concatenate(pieces, axis=1).astype(BF16)
    embed[...] = row_embed[: embed.shape[0]]
    classes, n_rows = table.shape[0], icl_in.shape[0]
    number = lax.broadcasted_iota(jnp.int32, (classes, n_rows), 0).astype(F32)
    hot = number == labels[0:1, :n_rows].astype(F32)
    hot = jnp.where(hot & (flags[0:1, :n_rows].astype(F32) == 1.0), 1.0, 0.0).astype(F32)
    label = lax.dot_general(hot, table[...].astype(F32), TN, preferred_element_type=F32)
    icl_in[...] = (row_embed.astype(F32) + label).astype(BF16)


def query_kernel(embed, icl_query, icl_kvo, turned_query):
    n_rows, full = embed.shape
    query = dot(embed[...], icl_query[...]).astype(BF16)
    head = full // HEADS
    scale = LOG2E / math.sqrt(head)
    for h in range(HEADS):
        lanes = slice(h * head, (h + 1) * head)
        turned_query[h * n_rows : (h + 1) * n_rows] = (
            dot_nt(query[:, lanes], icl_kvo[0, :, lanes]) * scale
        ).astype(BF16)


def icl_kernel(order, *refs):
    parts, (turned_query, mask_row, embed, icl_kvo, out) = sort_refs(refs, order)
    rows = jnp.concatenate([r[...] for r in parts], axis=0)
    full = rows.shape[1]
    n_rows = embed.shape[0]
    head = full // HEADS
    s = dot_nt(turned_query[...], rows)
    s = jnp.where(mask_row[0:1] > 0.5, s, -1e30)
    p = jnp.exp2(s - jnp.max(s, axis=1, keepdims=True))
    denom = jnp.sum(p, axis=1, keepdims=True)
    y = (dot(p.astype(BF16), rows) / denom).astype(BF16)
    mix = jnp.concatenate(
        [
            dot(y[h * n_rows : (h + 1) * n_rows], icl_kvo[1, :, h * head : (h + 1) * head])
            for h in range(HEADS)
        ],
        axis=1,
    ).astype(BF16)
    out[...] = (embed[...].astype(F32) + dot(mix, icl_kvo[2])).astype(BF16)


def call(kernel, outs, *args, scratch=(), mib=16, cost=None, name=None):
    return pl.pallas_call(
        kernel,
        out_shape=tuple(jax.ShapeDtypeStruct(s, d) for s, d in outs),
        in_specs=[pl.BlockSpec(memory_space=pltpu.VMEM)] * len(args),
        out_specs=tuple(pl.BlockSpec(memory_space=pltpu.VMEM) for _ in outs),
        scratch_shapes=scratch,
        compiler_params=pltpu.CompilerParams(vmem_limit_bytes=mib * 1024 * 1024),
        cost_estimate=cost,
        name=name,
    )(*args)


def swap(x, distance):
    n_dev = lax.axis_size("row")
    return lax.ppermute(x, "row", [(s, s ^ distance) for s in range(n_dev)])


CHUNKS = (8, 8)
HEAD_STEP = 2
P_SLOTS = 8
ORDER = (2, 6, 3, 4, 5, 7, 1)
Z_ORDER = (2, 3, 1)


def on_device(
    cells,
    is_context,
    labels,
    inducing,
    induce_query,
    column_kvo,
    cell_qkvo,
    class_tokens,
    class_query,
    row_kvo,
    label_table,
    icl_query,
    icl_kvo,
):
    n_rows, n_feat, width = cells.shape
    n_induce = inducing.shape[0]
    n_class = class_tokens.shape[0]
    n_dev = lax.axis_size("row")
    n_split = lax.axis_size("feat")
    own_feat = n_feat // n_dev
    n_total = n_dev * n_rows
    local_rows = n_rows // n_split
    full = n_class * width
    n_weights = n_class * ROW_HEADS
    paired = n_split == 1 and n_dev == 16 and n_rows * n_class == width

    head = n_rows // 2
    chunks = CHUNKS if paired and sum(CHUNKS) == own_feat else (own_feat,)
    chips = n_dev // 2
    groups = []
    if paired:
        order = (0,) + ORDER
        at = 0
        notes = jnp.stack([is_context, labels])
        for c, n in enumerate(chunks):
            top = 0 if c else head
            keep, send = call(
                functools.partial(pack_kernel, "row", n, own_feat, at, c == 0),
                [((chips, top + n * n_rows, width), BF16)] * 2,
                cells, *(() if c else (notes,)),
                mib=8, name="pack",
            )
            got = swap(send, 1)
            both = jnp.stack([keep, got], axis=1)
            groups.append([both[:1]] + [swap(both[q : q + 1], 2 * q) for q in ORDER])
            at += n
    else:
        order = (0,)
        by_feat = jnp.transpose(cells, (1, 0, 2)).reshape(n_dev, own_feat * n_rows, width)
        flags = jnp.where(is_context == 1, 1.0, 0.0).astype(BF16).reshape(2, head)
        tile = jnp.repeat(flags.T, width // 2, axis=1)
        payload = jnp.concatenate(
            [jnp.broadcast_to(tile[None], (n_dev,) + tile.shape), by_feat], axis=1
        )
        got = lax.all_to_all(payload, "row", split_axis=0, concat_axis=0, tiled=True)
        groups.append([got[:, None]])

    inducing, _ = lax.optimization_barrier((inducing, groups[0][0]))
    prepared = call(
        prep_kernel,
        [
            ((HEADS * n_induce, width), BF16),
            ((HEADS * width, 2 * HEADS * width), BF16),
            ((n_induce, 2 * HEADS * width), F32),
            ((n_weights + width, width), BF16),
            ((2, n_class, width), F32),
        ],
        inducing, induce_query, column_kvo, cell_qkvo, class_tokens, class_query, row_kvo,
        name="prep",
    )
    folded, cls_sums = prepared[:4], prepared[4]

    mask, mask_row, label_row = call(
        functools.partial(notes_kernel, order, head),
        [((n_total, width), BF16), ((8, n_total), F32), ((8, n_total), F32)],
        *groups[0],
        name="notes",
    )
    state = ()
    lines = width + ROW_HEADS
    sent = (n_dev, lines, width) if paired else (n_total, full + width)
    for c, n in enumerate(chunks):
        last = c == len(chunks) - 1
        state = call(
            functools.partial(
                column_kernel, order, n, n_rows, 0 if c else head, c == 0, last, paired
            ),
            [(sent, BF16) if last else ((full + n_weights, n_total), F32)],
            *groups[c], *state, *folded, mask,
            scratch=[
                pltpu.VMEM((n, width, n_total), BF16),
                pltpu.VMEM((n * n_induce, HEADS * width), BF16),
                pltpu.VMEM((n, 2 * HEADS * n_induce, width), BF16),
                pltpu.VMEM((P_SLOTS, HEADS * n_induce, math.gcd(n_total, 512)), BF16),
                pltpu.VMEM((n, n_weights, n_total), F32),
                pltpu.VMEM((n, width, n_total), F32),
            ],
            mib=24,
            cost=pl.CostEstimate(
                flops=n * n_total * width * 4000, transcendentals=0, bytes_accessed=4 * 1024 * 1024
            ),
            name="column",
        )
    (partial,) = state

    if paired:
        half = partial.reshape(2, chips, lines, width)
        (sums,) = call(
            sum_kernel, [(half.shape[1:], BF16)], half[0], swap(half[1], 1), name="sum"
        )
        sums = sums.reshape(chips // 2, 2, lines, width)
        (own,) = call(
            sum_kernel,
            [(sums.shape[1:], BF16)],
            sums[0], *[swap(sums[z], 4 * z) for z in Z_ORDER],
            name="sum",
        )
        other = swap(own, 2)
        own_flags, own_labels, near = mask_row, label_row, 2 * n_rows
    else:
        own = lax.all_to_all(
            partial.reshape(n_dev * n_split, local_rows, full + width),
            ("row", "feat"), split_axis=0, concat_axis=0, tiled=True,
        )
        other = cls_sums
        own_flags = lax.dynamic_slice_in_dim(
            is_context, lax.axis_index("feat") * local_rows, local_rows
        ).reshape(1, local_rows)
        own_labels, near = labels.reshape(1, local_rows), local_rows
    embed, icl_in = call(
        functools.partial(row_kernel, paired),
        [((local_rows, full), BF16), ((near, full), BF16)],
        own, other, own_flags, own_labels, cls_sums, class_tokens, row_kvo, label_table,
        name="row",
    )
    if paired:
        z_order = (0,) + Z_ORDER
        mine = [icl_in] + [swap(icl_in, 4 * z) for z in Z_ORDER]
        rows = mine + [swap(r, 1) for r in mine]
        row_order = z_order + tuple(chips // 2 + z for z in z_order)
    else:
        rows = (lax.all_gather(icl_in, ("row", "feat"), axis=0, tiled=True),)
        row_order = (0,)
    (turned_query,) = call(
        query_kernel,
        [((HEADS * local_rows, full), BF16)],
        embed, icl_query, icl_kvo,
        name="query",
    )
    (out,) = call(
        functools.partial(icl_kernel, row_order),
        [((local_rows, full), BF16)],
        *rows, turned_query, mask_row, embed, icl_kvo,
        name="icl",
    )
    return out


def solution(mesh):
    return jax.shard_map(
        on_device,
        mesh=mesh,
        in_specs=(
            P(("group", "row"), "feat", None),
            P(("group", "row")),
            P(("group", "row", "feat")),
            P(), P(), P(), P(), P(), P(), P(), P(), P(), P(),
        ),
        out_specs=P(("group", "row", "feat"), None),
        check_vma=False,
    )
```
